256 devices in a mesh: enc: 16 (over z, core), seq: 16 (over y, x).
Axes of the slice: x: 4, y: 4, z: 8, core: 2. Of those that a mesh axis runs over, the one named last changes fastest.
Arguments:
- queries: bfloat16 [16, 2048, 8192], P('enc', 'seq'), may hold values from -160 to 160
- kv_pool: bfloat16 [128, 2, 128, 8192], P('enc', None, None, 'seq'), may hold values from -16 to 16
- send_lists: int32 [16, 16, 1], P('enc'), may hold values from 0 to 7, as said below
- block_slots: int32 [16, 32, 2], P('enc'), may hold values from 0 to 15, as said below
- grad_context: bfloat16 [16, 2048, 8192], P('enc', 'seq'), may hold values from -24 to 24
Outputs:
- context: bfloat16 [16, 2048, 8192], P('enc', 'seq')
- grad_queries: bfloat16 [16, 2048, 8192], P('enc', 'seq')
- grad_pool: bfloat16 [128, 2, 128, 8192], P('enc', None, None, 'seq')
The draws below stay inside these ranges and needn't reach their ends.
Inputs may be any that keep to these rules, and one draw needn't show every extreme that they name: send_lists[o, e] names 1 different local entries; each of a shard's 8 entries is named for at least one sequence. `block_slots`: the two slots of a block differ; every slot of a sequence is named by at least one of its blocks.
All inputs are finite; a program needn't handle non-finite values.
Results may differ from the reference program's by a relative error of at most 0.0065.
Values may be sent and summed in bfloat16 or wider, within the bound.
A program may use at most 128 MiB of HBM per device.

```python
import math
import jax
import jax.numpy as jnp
from jax import lax

HEADS = 64
DH = 128
BLOCK = 64
CAP = 1
NBLEN = 128
SEQS = 16
SEQLEN = 2048
BLOCKS = 32
SLOTS = 16
POOL = 8
POOLS = 128


def draw_queries(key, part):
    first_key, scale_key = jax.random.split(key, 2)
    shape = (SEQS, SEQLEN, HEADS, DH)
    values = jnp.clip(jax.random.normal(first_key, shape, jnp.float32), -6.0, 6.0)
    row_scale = jnp.exp(jax.random.uniform(scale_key, (SEQS, SEQLEN, HEADS, 1), jnp.float32, math.log(0.4), math.log(2.5)))
    values = values * row_scale
    return values.reshape(SEQS, SEQLEN, HEADS * DH).astype(jnp.bfloat16)


def draw_kv_pool(key, part):
    first_key, scale_key = jax.random.split(key, 2)
    shape = (POOLS, 2, NBLEN, HEADS, DH)
    values = jnp.clip(jax.random.normal(first_key, shape, jnp.float32), -6.0, 6.0)
    row_scale = jnp.exp(jax.random.uniform(scale_key, (POOLS, 2, NBLEN, HEADS, 1), jnp.float32, math.log(0.4), math.log(2.5)))
    values = values * row_scale
    return values.reshape(POOLS, 2, NBLEN, HEADS * DH).astype(jnp.bfloat16)


def draw_send_lists(key, part):
    owner_keys = jax.random.split(jax.random.fold_in(key, 7), SEQS)

    def one_owner(owner_key):
        first_key, order_key = jax.random.split(owner_key)
        first_entry = jax.random.permutation(first_key, SEQS) % POOL
        orders = jax.vmap(lambda sub_key: jax.random.permutation(sub_key, POOL))(jax.random.split(order_key, SEQS))
        where_first = jnp.argmax(orders == first_entry[:, None], axis=1)
        picked = (where_first[:, None] + jnp.arange(CAP)[None, :]) % POOL
        return jnp.take_along_axis(orders, picked, axis=1)
    return jax.vmap(one_owner)(owner_keys).astype(jnp.int32)


def draw_block_slots(key, part):
    sequence_keys = jax.random.split(jax.random.fold_in(key, 9), SEQS)

    def one_sequence(sequence_key):
        first_key, step_key = jax.random.split(sequence_key)
        first_slot = jax.random.permutation(first_key, BLOCKS) % SLOTS
        step_size = jax.random.randint(step_key, (BLOCKS,), 1, SLOTS)
        return jnp.stack([first_slot, (first_slot + step_size) % SLOTS], axis=1)
    return jax.vmap(one_sequence)(sequence_keys).astype(jnp.int32)


def block_scale(rng, extent, cuts, least, largest):
    factor_of = 1.0
    for position, parts in cuts:
        steps = jax.random.uniform(jax.random.fold_in(jax.random.fold_in(rng, 6), position), (parts,), jnp.float32, least / len(cuts), largest / len(cuts))
        factor_of = factor_of * jnp.repeat(jnp.exp(steps), extent[position] // parts).reshape((-1,) + (1,) * (len(extent) - 1 - position))
    return factor_of


def gaussian(rng, extent, deviation, limit, pieces=(), kind=jnp.bfloat16):
    array = deviation * jax.random.normal(rng, extent, jnp.float32)
    if pieces:
        array = array * block_scale(rng, extent, pieces, -0.22, 0.18)
    return jnp.clip(array, -limit, limit).astype(kind)


def setup_inputs(seed: int = 0) -> dict:
    splits = jax.random.split(jax.random.key(seed), 6)
    return {
        "queries": draw_queries(jax.random.fold_in(splits[5], 71), 0),
        "kv_pool": draw_kv_pool(jax.random.fold_in(splits[5], 71), 0),
        "send_lists": draw_send_lists(jax.random.fold_in(splits[5], 71), 0),
        "block_slots": draw_block_slots(jax.random.fold_in(splits[5], 71), 0),
        "grad_context": gaussian(splits[4], (SEQS, SEQLEN, HEADS * DH), 4.0, 24.0, ((0, 16), (1, 16))),
    }


def move_up(row_data):
    filler = jnp.zeros((BLOCK - 1, row_data.shape[1]), row_data.dtype)
    return jnp.concatenate([row_data[BLOCK - 1:], filler], axis=0)


def move_down(row_data):
    filler = jnp.zeros((BLOCK - 1, row_data.shape[1]), row_data.dtype)
    return jnp.concatenate([filler, row_data[:row_data.shape[0] - BLOCK + 1]], axis=0)


def one_sequence(query_rows, received, block_use, grad_rows):
    head_width = query_rows.shape[1]
    heads_all = head_width // DH
    score_scale = DH ** -0.5
    best = lax.Precision.HIGHEST
    queries_moved = move_up(query_rows).reshape(BLOCKS, BLOCK, heads_all, DH).astype(jnp.float32)
    keys_used = received[block_use, 0].reshape(BLOCKS, 2 * NBLEN, heads_all, DH).astype(jnp.float32)
    values_used = received[block_use, 1].reshape(BLOCKS, 2 * NBLEN, heads_all, DH).astype(jnp.float32)
    scores = jnp.einsum("cihd,cjhd->chij", queries_moved, keys_used, precision=best) * score_scale
    row_peak = jnp.max(scores, axis=-1, keepdims=True)
    weights = jnp.exp(scores - row_peak)
    row_probs = weights / jnp.sum(weights, axis=-1, keepdims=True)
    probs_low = lax.optimization_barrier(row_probs.astype(jnp.bfloat16))
    out_blocks = jnp.einsum("chij,cjhd->cihd", probs_low.astype(jnp.float32), values_used, precision=best).astype(jnp.bfloat16)
    context = move_down(out_blocks.reshape(SEQLEN, head_width))
    grads_moved = move_up(grad_rows).reshape(BLOCKS, BLOCK, heads_all, DH).astype(jnp.float32)
    grad_probs = jnp.einsum("cihd,cjhd->chij", grads_moved, values_used, precision=best)
    row_inner = jnp.sum(row_probs * grad_probs, axis=-1, keepdims=True)
    grad_scores = lax.optimization_barrier((row_probs * (grad_probs - row_inner) * score_scale).astype(jnp.bfloat16))
    grad_wide = grad_scores.astype(jnp.float32)
    query_grads = jnp.einsum("chij,cjhd->cihd", grad_wide, keys_used, precision=best).astype(jnp.bfloat16)
    grad_queries = move_down(query_grads.reshape(SEQLEN, head_width))
    key_grads = jnp.einsum("chij,cihd->cjhd", grad_wide, queries_moved, precision=best)
    value_grads = jnp.einsum("chij,cihd->cjhd", probs_low.astype(jnp.float32), grads_moved, precision=best)
    use_grads = jnp.stack([key_grads.reshape(BLOCKS, 2, NBLEN, head_width), value_grads.reshape(BLOCKS, 2, NBLEN, head_width)], axis=2)
    use_grads = use_grads.reshape(BLOCKS * 2, 2, NBLEN, head_width)
    use_low = lax.optimization_barrier(use_grads.astype(jnp.bfloat16)).astype(jnp.float32)
    slot_grads = jax.ops.segment_sum(use_low, block_use.reshape(-1), num_segments=SLOTS).astype(jnp.bfloat16)
    return context, grad_queries, slot_grads


def reference(queries, kv_pool, send_lists, block_slots, grad_context):
    owner_base = jnp.arange(SEQS, dtype=jnp.int32)[:, None] * POOL

    def per_sequence(pool_sum, sequence):
        pool_rows = (owner_base + send_lists[:, sequence, :]).reshape(-1).astype(jnp.int32)
        received = kv_pool[pool_rows]
        context, grad_queries, slot_grads = one_sequence(queries[sequence], received, block_slots[sequence], grad_context[sequence])
        slot_wide = lax.optimization_barrier(slot_grads).astype(jnp.float32)
        pool_sum = pool_sum.at[pool_rows].add(slot_wide)
        return pool_sum, (context, grad_queries)

    start = jnp.zeros(kv_pool.shape, jnp.float32)
    pool_sum, outputs = lax.scan(per_sequence, start, jnp.arange(SEQS, dtype=jnp.int32))
    return outputs[0], outputs[1], pool_sum.astype(jnp.bfloat16)
```

```python
import functools

import jax
import jax.numpy as jnp
from jax import lax
from jax.experimental import pallas as pl
from jax.experimental.pallas import tpu as pltpu
from jax.sharding import PartitionSpec as P

DH = 128
BLOCK = 64
NBLEN = 128
MESH = pl.DeviceIdType.MESH
ANY = pl.BlockSpec(memory_space=pl.ANY)
SCALAR = pl.BlockSpec(memory_space=pltpu.SMEM)
MIB = 1 << 20


def greet(enc_count, seq_count, enc_here, seq_here):
    barrier = pltpu.get_barrier_semaphore()
    for k in range(1, enc_count):
        peer = lax.rem(enc_here + k, enc_count)
        pl.semaphore_signal(barrier, inc=1, device_id={"enc": peer}, device_id_type=MESH)
    for k in range(1, seq_count):
        peer = lax.rem(seq_here + k, seq_count)
        pl.semaphore_signal(barrier, inc=1, device_id={"seq": peer}, device_id_type=MESH)
    return barrier


def remote(source, target, sems, which, axis, peer):
    return pltpu.make_async_remote_copy(
        src_ref=source,
        dst_ref=target,
        send_sem=sems.at[0, which],
        recv_sem=sems.at[1, which],
        device_id={axis: peer},
        device_id_type=MESH,
    )


def gather_kernel(
    enc_count, seq_count, entries, queries, grads, pool, head_queries, head_grads, arrived,
    outgoing, enc_sems, query_sems, grad_sems, own_sems,
):
    enc_here, seq_here = lax.axis_index("enc"), lax.axis_index("seq")
    rows, width = queries.shape[0], pool.shape[-1]
    barrier = greet(enc_count, seq_count, enc_here, seq_here)

    def pick(e, carry):
        outgoing[e] = pool[entries[e]]
        return carry

    lax.fori_loop(0, enc_count, pick, 0)
    pl.semaphore_wait(barrier, enc_count + seq_count - 2)

    copies = []
    far = enc_count // 2
    for k in sorted(range(1, enc_count), key=lambda k: -min(k, enc_count - k)):
        peer = lax.rem(enc_here + k, enc_count)
        copies.append(remote(outgoing.at[peer], arrived.at[enc_here], enc_sems, k, "enc", peer))
        copies[-1].start()
    mine = pl.ds(pl.multiple_of(seq_here * rows, rows), rows)
    for source, target, sems in ((queries, head_queries, query_sems), (grads, head_grads, grad_sems)):
        for k in range(1, seq_count):
            peer = lax.rem(seq_here + k, seq_count)
            part = pl.ds(pl.multiple_of(peer * width, width), width)
            copies.append(remote(source.at[:, part], target.at[mine, :], sems, k, "seq", peer))
            copies[-1].start()
    part = pl.ds(pl.multiple_of(seq_here * width, width), width)
    for n, (source, target) in enumerate((
        (outgoing.at[enc_here], arrived.at[enc_here]),
        (queries.at[:, part], head_queries.at[mine, :]),
        (grads.at[:, part], head_grads.at[mine, :]),
    )):
        copies.append(pltpu.make_async_copy(source, target, own_sems.at[n]))
        copies[-1].start()
    for copy in copies:
        copy.wait()


def gather(enc_count, seq_count, entries, queries, grads, pool):
    rows, width = queries.shape[0], pool.shape[-1]
    heads = jax.ShapeDtypeStruct((rows * seq_count, width), queries.dtype)
    received = (enc_count,) + pool.shape[1:]
    return pl.pallas_call(
        functools.partial(gather_kernel, enc_count, seq_count),
        out_shape=(heads, heads, jax.ShapeDtypeStruct(received, pool.dtype)),
        in_specs=[SCALAR, ANY, ANY, pl.BlockSpec(memory_space=pltpu.VMEM)],
        out_specs=(ANY, ANY, ANY),
        scratch_shapes=[
            pltpu.VMEM(received, pool.dtype),
            pltpu.SemaphoreType.DMA((2, enc_count)),
            pltpu.SemaphoreType.DMA((2, seq_count)),
            pltpu.SemaphoreType.DMA((2, seq_count)),
            pltpu.SemaphoreType.DMA((3,)),
        ],
        compiler_params=pltpu.CompilerParams(
            collective_id=0, has_side_effects=True, vmem_limit_bytes=24 * MIB
        ),
    )(entries, queries, grads, pool)


def attend_kernel(slots, queries, grads, received, context, grad_queries, slot_grads, total):
    blocks = queries.shape[0] // BLOCK
    scale = DH ** (-0.5)
    total[...] = jnp.zeros_like(total)
    is_last = lax.broadcasted_iota(jnp.int32, (BLOCK, 2 * DH), 0) == BLOCK - 1
    is_first_head = lax.broadcasted_iota(jnp.int32, (BLOCK, 2 * DH), 1) < DH
    nt = (((1,), (1,)), ((), ()))
    tn = (((0,), (0,)), ((), ()))
    f32 = jnp.float32

    def moved(ref, b):
        here = ref[pl.ds(pl.multiple_of(b * BLOCK, BLOCK), BLOCK), :].astype(f32)
        after = jnp.minimum(b + 1, blocks - 1)
        later = ref[pl.ds(pl.multiple_of(after * BLOCK, BLOCK), BLOCK), :].astype(f32)
        later = jnp.where(b + 1 < blocks, later, 0.0)
        row = jnp.where(is_last, here, later)
        pair = [jnp.where(is_first_head, row, 0.0), jnp.where(is_first_head, 0.0, row)]
        return jnp.concatenate(pair, axis=0).astype(jnp.bfloat16)

    def both(wide):
        return jnp.where(is_first_head, wide[:BLOCK], wide[BLOCK:])

    def step(b, carry):
        last_out, last_grad = carry
        first, second = slots[2 * b], slots[2 * b + 1]
        query, grad = moved(queries, b), moved(grads, b)
        keys = jnp.concatenate([received[first, 0], received[second, 0]], axis=0)
        values = jnp.concatenate([received[first, 1], received[second, 1]], axis=0)
        scores = lax.dot_general(query, keys, nt, preferred_element_type=f32) * scale
        weights = jnp.exp(scores - jnp.max(scores, axis=-1, keepdims=True))
        probs = weights * (1.0 / jnp.sum(weights, axis=-1, keepdims=True))
        probs_low = probs.astype(jnp.bfloat16)
        out = both(jnp.dot(probs_low, values, preferred_element_type=f32))
        grad_probs = lax.dot_general(grad, values, nt, preferred_element_type=f32)
        inner = jnp.sum(probs * grad_probs, axis=-1, keepdims=True)
        grad_scores = (probs * (grad_probs - inner) * scale).astype(jnp.bfloat16)
        query_grad = both(jnp.dot(grad_scores, keys, preferred_element_type=f32))
        key_grad = lax.dot_general(grad_scores, query, tn, preferred_element_type=f32)
        value_grad = lax.dot_general(probs_low, grad, tn, preferred_element_type=f32)
        total[first, 0] += key_grad[:NBLEN]
        total[first, 1] += value_grad[:NBLEN]
        total[second, 0] += key_grad[NBLEN:]
        total[second, 1] += value_grad[NBLEN:]
        here = pl.ds(pl.multiple_of(b * BLOCK, BLOCK), BLOCK)
        context[here, :] = jnp.where(is_last, out, last_out).astype(context.dtype)
        grad_queries[here, :] = jnp.where(is_last, query_grad, last_grad).astype(context.dtype)
        return out, query_grad

    zeros = jnp.zeros((BLOCK, 2 * DH), f32)
    lax.fori_loop(0, blocks, step, (zeros, zeros), unroll=2)
    slot_grads[...] = total[...].astype(slot_grads.dtype)


def attend(slots, head_queries, head_grads, received):
    length, width = head_queries.shape
    entries = received.shape[0]
    pair = 2 * DH
    rows = pl.BlockSpec((length, pair), lambda h: (0, h))
    pool = pl.BlockSpec((entries, 2, NBLEN, pair), lambda h: (0, 0, 0, h))
    return pl.pallas_call(
        attend_kernel,
        out_shape=(
            jax.ShapeDtypeStruct(head_queries.shape, head_queries.dtype),
            jax.ShapeDtypeStruct(head_queries.shape, head_queries.dtype),
            jax.ShapeDtypeStruct(received.shape, received.dtype),
        ),
        grid=(width // pair,),
        in_specs=[SCALAR, rows, rows, pool],
        out_specs=(rows, rows, pool),
        scratch_shapes=[pltpu.VMEM((entries, 2, NBLEN, pair), jnp.float32)],
        compiler_params=pltpu.CompilerParams(vmem_limit_bytes=40 * MIB),
    )(slots, head_queries, head_grads, received)


def scatter_kernel(
    enc_count, seq_count, head_context, head_grads, slot_grads, context, grad_queries, returned,
    enc_sems, context_sems, grad_sems, own_sems,
):
    enc_here, seq_here = lax.axis_index("enc"), lax.axis_index("seq")
    rows, width = context.shape[0], head_context.shape[1]
    barrier = greet(enc_count, seq_count, enc_here, seq_here)
    pl.semaphore_wait(barrier, enc_count + seq_count - 2)
    copies = []
    for k in sorted(range(1, enc_count), key=lambda k: -min(k, enc_count - k)):
        peer = lax.rem(enc_here + k, enc_count)
        copies.append(remote(slot_grads.at[peer], returned.at[enc_here], enc_sems, k, "enc", peer))
        copies[-1].start()
    part = pl.ds(pl.multiple_of(seq_here * width, width), width)
    for source, target, sems in ((head_context, context, context_sems), (head_grads, grad_queries, grad_sems)):
        for k in range(1, seq_count):
            peer = lax.rem(seq_here + k, seq_count)
            theirs = pl.ds(pl.multiple_of(peer * rows, rows), rows)
            copies.append(remote(source.at[theirs, :], target.at[:, part], sems, k, "seq", peer))
            copies[-1].start()
    mine = pl.ds(pl.multiple_of(seq_here * rows, rows), rows)
    for n, (source, target) in enumerate((
        (slot_grads.at[enc_here], returned.at[enc_here]),
        (head_context.at[mine, :], context.at[:, part]),
        (head_grads.at[mine, :], grad_queries.at[:, part]),
    )):
        copies.append(pltpu.make_async_copy(source, target, own_sems.at[n]))
        copies[-1].start()
    for copy in copies:
        copy.wait()


def scatter(enc_count, seq_count, head_context, head_grads, slot_grads):
    length, width = head_context.shape
    tokens = jax.ShapeDtypeStruct((length // seq_count, width * seq_count), head_context.dtype)
    return pl.pallas_call(
        functools.partial(scatter_kernel, enc_count, seq_count),
        out_shape=(tokens, tokens, jax.ShapeDtypeStruct(slot_grads.shape, slot_grads.dtype)),
        in_specs=[ANY] * 3,
        out_specs=(ANY, ANY, ANY),
        scratch_shapes=[
            pltpu.SemaphoreType.DMA((2, enc_count)),
            pltpu.SemaphoreType.DMA((2, seq_count)),
            pltpu.SemaphoreType.DMA((2, seq_count)),
            pltpu.SemaphoreType.DMA((3,)),
        ],
        compiler_params=pltpu.CompilerParams(
            collective_id=1, has_side_effects=True, vmem_limit_bytes=4 * MIB
        ),
    )(head_context, head_grads, slot_grads)


def owner_kernel(entries, returned, context, grad_queries, pool_grads, context_out, grad_out, total, sems):
    moves = [
        pltpu.make_async_copy(context, context_out, sems.at[0]),
        pltpu.make_async_copy(grad_queries, grad_out, sems.at[1]),
    ]

    @pl.when(pl.program_id(0) == 0)
    def _():
        for move in moves:
            move.start()

    total[...] = jnp.zeros_like(total)

    def step(e, carry):
        total[entries[e]] += returned[e].astype(jnp.float32)
        return carry

    lax.fori_loop(0, returned.shape[0], step, 0)
    pool_grads[...] = total[...].astype(pool_grads.dtype)

    @pl.when(pl.program_id(0) == pl.num_programs(0) - 1)
    def _():
        for move in moves:
            move.wait()


def owner_sum(entries, returned, context, grad_queries, pool_shape):
    cuts = 4
    count, two, length, width = returned.shape
    part = length // cuts
    tokens = jax.ShapeDtypeStruct(context.shape, context.dtype)
    return pl.pallas_call(
        owner_kernel,
        out_shape=(jax.ShapeDtypeStruct(pool_shape, returned.dtype), tokens, tokens),
        grid=(cuts,),
        in_specs=[
            SCALAR,
            pl.BlockSpec((count, two, part, width), lambda i: (0, 0, i, 0)),
            ANY,
            ANY,
        ],
        out_specs=(pl.BlockSpec((pool_shape[0], two, part, width), lambda i: (0, 0, i, 0)), ANY, ANY),
        scratch_shapes=[
            pltpu.VMEM((pool_shape[0], two, part, width), jnp.float32),
            pltpu.SemaphoreType.DMA((2,)),
        ],
        compiler_params=pltpu.CompilerParams(vmem_limit_bytes=24 * MIB),
    )(entries, returned, context, grad_queries)


def local(enc_count, seq_count, queries, kv_pool, send_lists, block_slots, grad_context):
    entries = send_lists.reshape(-1)
    slots = block_slots.reshape(-1)
    head_queries, head_grads, received = gather(
        enc_count, seq_count, entries, queries[0], grad_context[0], kv_pool
    )
    head_context, head_query_grads, slot_grads = attend(slots, head_queries, head_grads, received)
    context, grad_queries, returned = scatter(
        enc_count, seq_count, head_context, head_query_grads, slot_grads
    )
    pool_grads, context, grad_queries = owner_sum(
        entries, returned, context, grad_queries, kv_pool.shape
    )
    return context[None], grad_queries[None], pool_grads


def solution(mesh):
    in_specs = (
        P("enc", "seq", None),
        P("enc", None, None, "seq"),
        P("enc", None, None),
        P("enc", None, None),
        P("enc", "seq", None),
    )
    out_specs = (P("enc", "seq", None), P("enc", "seq", None), P("enc", None, None, "seq"))
    body = functools.partial(local, mesh.shape["enc"], mesh.shape["seq"])
    return jax.shard_map(body, mesh=mesh, in_specs=in_specs, out_specs=out_specs, check_vma=False)
```

```python
import functools

import jax
import jax.numpy as jnp
from jax import lax
from jax.experimental import pallas as pl
from jax.experimental.pallas import tpu as pltpu
from jax.sharding import PartitionSpec as P

DH = 128
BLOCK = 64
NBLEN = 128
PAIR = 2 * DH
MESH = pl.DeviceIdType.MESH
ANY = pl.BlockSpec(memory_space=pl.ANY)
SCALAR = pl.BlockSpec(memory_space=pltpu.SMEM)
MIB = 1 << 20
NT = (((1,), (1,)), ((), ()))
TN = (((0,), (0,)), ((), ()))
F32 = jnp.float32
BF16 = jnp.bfloat16


def sort_kernel(slots, order, fresh, last, count):
    uses, entries = slots.shape[0], last.shape[0]

    def clear(s, carry):
        count[s] = 0
        return carry

    def tally(u, carry):
        count[slots[u]] += 1
        fresh[u] = 0
        return carry

    def starts(s, begin):
        size = count[s]
        count[s] = begin
        last[s] = begin + size - 1
        fresh[begin] = 1
        return begin + size

    def place(u, carry):
        slot = slots[u]
        order[count[slot]] = u
        count[slot] += 1
        return carry

    lax.fori_loop(0, entries, clear, 0)
    lax.fori_loop(0, uses, tally, 0)
    lax.fori_loop(0, entries, starts, 0)
    lax.fori_loop(0, uses, place, 0)


def sort_uses(slots, entries):
    uses = slots.shape[0]
    return pl.pallas_call(
        sort_kernel,
        out_shape=(
            jax.ShapeDtypeStruct((uses,), jnp.int32),
            jax.ShapeDtypeStruct((uses,), jnp.int32),
            jax.ShapeDtypeStruct((entries,), jnp.int32),
        ),
        in_specs=[SCALAR],
        out_specs=(SCALAR,) * 3,
        scratch_shapes=[pltpu.SMEM((entries,), jnp.int32)],
    )(slots)


def block_pass(slots, queries, grads, received, out, query_grads, wide_q, wide_g, probs_kept, scores_kept):
    blocks = queries.shape[0] // BLOCK
    scale = DH ** (-0.5)
    is_last = lax.broadcasted_iota(jnp.int32, (BLOCK, PAIR), 0) == BLOCK - 1
    is_first_head = lax.broadcasted_iota(jnp.int32, (BLOCK, PAIR), 1) < DH

    def moved(ref, b):
        here = ref[pl.ds(pl.multiple_of(b * BLOCK, BLOCK), BLOCK), :].astype(F32)
        after = jnp.minimum(b + 1, blocks - 1)
        later = ref[pl.ds(pl.multiple_of(after * BLOCK, BLOCK), BLOCK), :].astype(F32)
        later = jnp.where(b + 1 < blocks, later, 0.0)
        row = jnp.where(is_last, here, later)
        pair = [jnp.where(is_first_head, row, 0.0), jnp.where(is_first_head, 0.0, row)]
        return jnp.concatenate(pair, axis=0).astype(BF16)

    def both(wide):
        return jnp.where(is_first_head, wide[:BLOCK], wide[BLOCK:])

    def step(b, carry):
        last_out, last_grad = carry
        first, second = slots[2 * b], slots[2 * b + 1]
        query, grad = moved(queries, b), moved(grads, b)
        wide_q[b] = query
        wide_g[b] = grad
        keys = jnp.concatenate([received[first, 0], received[second, 0]], axis=0)
        values = jnp.concatenate([received[first, 1], received[second, 1]], axis=0)
        scores = lax.dot_general(query, keys, NT, preferred_element_type=F32) * scale
        weights = jnp.exp(scores - jnp.max(scores, axis=-1, keepdims=True))
        probs = weights * (1.0 / jnp.sum(weights, axis=-1, keepdims=True))
        probs_low = probs.astype(BF16)
        new_out = both(jnp.dot(probs_low, values, preferred_element_type=F32))
        grad_probs = lax.dot_general(grad, values, NT, preferred_element_type=F32)
        inner = jnp.sum(probs * grad_probs, axis=-1, keepdims=True)
        grad_scores = (probs * (grad_probs - inner) * scale).astype(BF16)
        new_grad = both(jnp.dot(grad_scores, keys, preferred_element_type=F32))
        for n in range(2):
            probs_kept[2 * b + n] = probs_low[:, n * NBLEN : (n + 1) * NBLEN]
            scores_kept[2 * b + n] = grad_scores[:, n * NBLEN : (n + 1) * NBLEN]
        here = pl.ds(pl.multiple_of(b * BLOCK, BLOCK), BLOCK)
        out[here, :] = jnp.where(is_last, new_out, last_out).astype(BF16)
        query_grads[here, :] = jnp.where(is_last, new_grad, last_grad).astype(BF16)
        return new_out, new_grad

    zeros = jnp.zeros((BLOCK, PAIR), F32)
    lax.fori_loop(0, blocks, step, (zeros, zeros), unroll=2)


def slot_pass(order, fresh, last, wide_q, wide_g, probs_kept, scores_kept, running, sums, slot_grads):
    sums[...] = jnp.zeros_like(sums)

    def step(u, carry):
        use = order[u]
        block = lax.div(use, 2)
        starts = fresh[u] == 1
        for part, (kept, wide) in enumerate(((scores_kept, wide_q), (probs_kept, wide_g))):
            new = lax.dot_general(kept[use], wide[block], TN, preferred_element_type=F32)
            new = jnp.where(starts, 0.0, sums[part]) + new
            sums[part] = new
            running[u, part] = new.astype(BF16)
        return carry

    def pick(s, carry):
        slot_grads[s] = running[last[s]]
        return carry

    lax.fori_loop(0, order.shape[0], step, 0, unroll=2)
    lax.fori_loop(0, slot_grads.shape[0], pick, 0)


def everything_kernel(
    enc_count, seq_count, chunks,
    entries, slots, order, fresh, last, queries, grads, pool, context, grad_queries, returned,
    *scratch,
):
    take = iter(scratch)
    per_chunk = [[next(take) for _ in range(8)] for _ in range(chunks)]
    wide_q, wide_g, probs_kept, scores_kept, running, sums = [next(take) for _ in range(6)]
    pool_sems, send_sems, recv_sems = [next(take) for _ in range(3)]

    enc_here, seq_here = lax.axis_index("enc"), lax.axis_index("seq")
    rows = queries.shape[0]
    width = pool.shape[-1]
    mine = pl.ds(pl.multiple_of(seq_here * rows, rows), rows)

    def peer_of(here, k, count):
        return lax.rem(here + k, count)

    loads = []
    for c in range(chunks):
        own = per_chunk[c][0]
        loads.append(pltpu.make_async_copy(pool.at[:, :, :, pl.ds(c * PAIR, PAIR)], own, pool_sems.at[c]))
        loads[-1].start()

    barrier = pltpu.get_barrier_semaphore()

    def greet_enc(k, carry):
        pl.semaphore_signal(
            barrier, inc=1, device_id={"enc": peer_of(enc_here, k, enc_count)}, device_id_type=MESH
        )
        return carry

    def greet_seq(k, carry):
        pl.semaphore_signal(
            barrier, inc=1, device_id={"seq": peer_of(seq_here, k, seq_count)}, device_id_type=MESH
        )
        return carry

    lax.fori_loop(1, enc_count, greet_enc, 0)
    lax.fori_loop(1, seq_count, greet_seq, 0)

    def pick(c):
        loads[c].wait()
        own, outgoing = per_chunk[c][0], per_chunk[c][1]

        def body(e, carry):
            outgoing[e] = own[entries[e]]
            return carry

        lax.fori_loop(0, enc_count, body, 0)

    def exchange(group, axis, here, count, source_of, target_of):
        def body(k, carry):
            peer = peer_of(here, k, count)
            pltpu.make_async_remote_copy(
                src_ref=source_of(peer),
                dst_ref=target_of(here),
                send_sem=send_sems.at[group],
                recv_sem=recv_sems.at[group],
                device_id={axis: peer},
                device_id_type=MESH,
            ).start()
            return carry

        lax.fori_loop(1, count, body, 0)
        pltpu.make_async_copy(source_of(here), target_of(here), recv_sems.at[group]).start()

    def cut(c, p):
        return pl.ds(pl.multiple_of(p * width + c * PAIR, PAIR), PAIR)

    def token_rows(p):
        return pl.ds(pl.multiple_of(p * rows, rows), rows)

    def fetch(c):
        own, outgoing, arrived = per_chunk[c][:3]
        exchange(6 * c, "enc", enc_here, enc_count, lambda p: outgoing.at[p], lambda p: arrived.at[p])

    def to_heads(c):
        head_queries, head_grads = per_chunk[c][3:5]
        for n, (source, target) in enumerate(((queries, head_queries), (grads, head_grads))):
            exchange(
                6 * c + 1 + n, "seq", seq_here, seq_count,
                lambda p, source=source: source.at[:, cut(c, p)],
                lambda p, target=target: target.at[token_rows(p), :],
            )

    def to_tokens(c):
        out, query_grads = per_chunk[c][5:7]
        for n, (source, target) in enumerate(((out, context), (query_grads, grad_queries))):
            exchange(
                6 * c + 3 + n, "seq", seq_here, seq_count,
                lambda p, source=source: source.at[token_rows(p), :],
                lambda p, target=target: target.at[:, cut(c, p)],
            )

    def give_back(c):
        slot_grads = per_chunk[c][7]
        exchange(
            6 * c + 5, "enc", enc_here, enc_count,
            lambda p: slot_grads.at[p], lambda p: returned.at[c, p],
        )

    def whole(ref, sem):
        pltpu.make_async_copy(ref, ref, sem).wait()

    def sent(group, ref, count):
        part = ref.at[pl.ds(0, ref.shape[0] // count * (count - 1))]
        whole(part, send_sems.at[group])

    def arrive(group, ref):
        whole(ref, recv_sems.at[group])

    def compute(c):
        _, _, arrived, head_queries, head_grads, out, query_grads, slot_grads = per_chunk[c]
        arrive(6 * c, arrived)
        arrive(6 * c + 1, head_queries)
        arrive(6 * c + 2, head_grads)
        block_pass(
            slots, head_queries, head_grads, arrived, out, query_grads,
            wide_q, wide_g, probs_kept, scores_kept,
        )
        to_tokens(c)
        slot_pass(
            order, fresh, last, wide_q, wide_g, probs_kept, scores_kept, running, sums, slot_grads
        )

    pick(0)
    pl.semaphore_wait(barrier, enc_count + seq_count - 2)
    fetch(0)
    to_heads(0)
    for c in range(1, chunks):
        pick(c)
    for c in range(chunks):
        sent(6 * c, per_chunk[c][1], enc_count)
        if c + 1 < chunks:
            fetch(c + 1)
            to_heads(c + 1)
        if c > 0:
            give_back(c - 1)
        compute(c)
    give_back(chunks - 1)

    for c in range(chunks):
        _, _, arrived, head_queries, head_grads, out, query_grads, slot_grads = per_chunk[c]
        sent(6 * c + 1, head_queries, seq_count)
        sent(6 * c + 2, head_grads, seq_count)
        sent(6 * c + 3, out, seq_count)
        sent(6 * c + 4, query_grads, seq_count)
        sent(6 * c + 5, slot_grads, enc_count)
        arrive(6 * c + 3, out)
        arrive(6 * c + 4, query_grads)
        arrive(6 * c + 5, slot_grads)


def everything(enc_count, seq_count, entries, slots, order, fresh, last, queries, grads, pool):
    rows = queries.shape[0]
    held, _, _, width = pool.shape
    chunks = width // PAIR
    length = rows * seq_count
    blocks = length // BLOCK
    tokens = jax.ShapeDtypeStruct(queries.shape, queries.dtype)

    def entry_buffer(count):
        return pltpu.VMEM((count, 2, NBLEN, PAIR), BF16)

    heads = pltpu.VMEM((length, PAIR), BF16)
    chunk_shapes = [
        entry_buffer(held), entry_buffer(enc_count), entry_buffer(enc_count),
        heads, heads, heads, heads, entry_buffer(enc_count),
    ]
    return pl.pallas_call(
        functools.partial(everything_kernel, enc_count, seq_count, chunks),
        out_shape=(
            tokens,
            tokens,
            jax.ShapeDtypeStruct((chunks, enc_count, 2, NBLEN, PAIR), pool.dtype),
        ),
        in_specs=[SCALAR] * 5 + [ANY] * 3,
        out_specs=(ANY, ANY, ANY),
        scratch_shapes=chunk_shapes * chunks
        + [
            pltpu.VMEM((blocks, 2 * BLOCK, PAIR), BF16),
            pltpu.VMEM((blocks, 2 * BLOCK, PAIR), BF16),
            pltpu.VMEM((2 * blocks, 2 * BLOCK, NBLEN), BF16),
            pltpu.VMEM((2 * blocks, 2 * BLOCK, NBLEN), BF16),
            pltpu.VMEM((2 * blocks, 2, NBLEN, PAIR), BF16),
            pltpu.VMEM((2, NBLEN, PAIR), F32),
            pltpu.SemaphoreType.DMA((chunks,)),
            pltpu.SemaphoreType.DMA((6 * chunks,)),
            pltpu.SemaphoreType.DMA((6 * chunks,)),
        ],
        compiler_params=pltpu.CompilerParams(
            collective_id=0, has_side_effects=True, vmem_limit_bytes=56 * MIB
        ),
    )(entries, slots, order, fresh, last, queries, grads, pool)


def owner_kernel(entries, returned, context, grad_queries, pool_grads, context_out, grad_out, total, sems):
    moves = [
        pltpu.make_async_copy(context, context_out, sems.at[0]),
        pltpu.make_async_copy(grad_queries, grad_out, sems.at[1]),
    ]
    step_here = pl.program_id(0) * pl.num_programs(1) + pl.program_id(1)

    @pl.when(step_here == 0)
    def _():
        for move in moves:
            move.start()

    total[...] = jnp.zeros_like(total)

    def step(e, carry):
        total[entries[e]] += returned[e].astype(F32)
        return carry

    lax.fori_loop(0, returned.shape[0], step, 0)
    pool_grads[...] = total[...].astype(pool_grads.dtype)

    @pl.when(step_here == pl.num_programs(0) * pl.num_programs(1) - 1)
    def _():
        for move in moves:
            move.wait()


def owner_sum(entries, returned, context, grad_queries, pool_shape):
    cuts = 2
    chunks, count, two, length, width = returned.shape
    part = length // cuts
    tokens = jax.ShapeDtypeStruct(context.shape, context.dtype)
    return pl.pallas_call(
        owner_kernel,
        out_shape=(jax.ShapeDtypeStruct(pool_shape, returned.dtype), tokens, tokens),
        grid=(chunks, cuts),
        in_specs=[
            SCALAR,
            pl.BlockSpec((None, count, two, part, width), lambda c, i: (c, 0, 0, i, 0)),
            ANY,
            ANY,
        ],
        out_specs=(pl.BlockSpec((pool_shape[0], two, part, width), lambda c, i: (0, 0, i, c)), ANY, ANY),
        scratch_shapes=[
            pltpu.VMEM((pool_shape[0], two, part, width), F32),
            pltpu.SemaphoreType.DMA((2,)),
        ],
        compiler_params=pltpu.CompilerParams(vmem_limit_bytes=58 * MIB),
    )(entries, returned, context, grad_queries)


def local(enc_count, seq_count, queries, kv_pool, send_lists, block_slots, grad_context):
    entries = send_lists.reshape(-1)
    slots = block_slots.reshape(-1)
    order, fresh, last = sort_uses(slots, enc_count)
    context, grad_queries, returned = everything(
        enc_count, seq_count, entries, slots, order, fresh, last, queries[0], grad_context[0], kv_pool
    )
    pool_grads, context, grad_queries = owner_sum(
        entries, returned, context, grad_queries, kv_pool.shape
    )
    return context[None], grad_queries[None], pool_grads


def solution(mesh):
    in_specs = (
        P("enc", "seq", None),
        P("enc", None, None, "seq"),
        P("enc", None, None),
        P("enc", None, None),
        P("enc", "seq", None),
    )
    out_specs = (P("enc", "seq", None), P("enc", "seq", None), P("enc", None, None, "seq"))
    body = functools.partial(local, mesh.shape["enc"], mesh.shape["seq"])
    return jax.shard_map(body, mesh=mesh, in_specs=in_specs, out_specs=out_specs, check_vma=False)
```

```python
import functools

import jax
import jax.numpy as jnp
from jax import lax
from jax.experimental import pallas as pl
from jax.experimental.pallas import tpu as pltpu
from jax.sharding import PartitionSpec as P

DH = 128
BLOCK = 64
NBLEN = 128
PAIR = 2 * DH
MESH = pl.DeviceIdType.MESH
ANY = pl.BlockSpec(memory_space=pl.ANY)
SCALAR = pl.BlockSpec(memory_space=pltpu.SMEM)
MIB = 1 << 20
NT = (((1,), (1,)), ((), ()))
TN = (((0,), (0,)), ((), ()))
F32 = jnp.float32
BF16 = jnp.bfloat16


def sort_uses(slots, rank_ref, ranks, sem):
    neighbours, blocks = slots.shape
    uses = neighbours * blocks
    lane = lax.broadcasted_iota(jnp.int32, (uses, 128), 1)
    row = lax.broadcasted_iota(jnp.int32, (uses, 128), 0)
    along_lanes = jnp.full((uses, 128), uses * 128, jnp.int32)
    along_rows = jnp.zeros((uses, 128), jnp.int32)
    slot_rows = jnp.zeros((uses, 128), jnp.int32)
    for n in range(neighbours):

        def put(b, carry, n=n):
            along_lanes, along_rows, slot_rows = carry
            use = n * blocks + b
            key = slots[n, b] * uses + use
            along_lanes = jnp.where(lane == use, key, along_lanes)
            along_rows = jnp.where(row == use, key, along_rows)
            slot_rows = jnp.where(row == use, slots[n, b], slot_rows)
            return along_lanes, along_rows, slot_rows

        along_lanes, along_rows, slot_rows = lax.fori_loop(
            0, blocks, put, (along_lanes, along_rows, slot_rows)
        )
    rank = jnp.sum((along_lanes < along_rows).astype(jnp.int32), axis=1, keepdims=True)
    order = jnp.sum(jnp.where(rank == lane, row, 0), axis=0, keepdims=True)
    ends = jnp.sum((slot_rows <= lane).astype(jnp.int32), axis=0, keepdims=True) - 1
    rank_ref[0:1, :] = order
    rank_ref[1:2, :] = ends
    copy = pltpu.make_async_copy(rank_ref, ranks, sem)
    copy.start()
    copy.wait()


def block_pass(slots, queries, grads, received, out, query_grads, wide_q, wide_g, probs_kept, scores_kept):
    blocks = queries.shape[0] // BLOCK
    scale = DH ** (-0.5)
    is_last = lax.broadcasted_iota(jnp.int32, (BLOCK, PAIR), 0) == BLOCK - 1
    is_first_head = lax.broadcasted_iota(jnp.int32, (BLOCK, PAIR), 1) < DH

    def moved(ref, b):
        here = ref[pl.ds(pl.multiple_of(b * BLOCK, BLOCK), BLOCK), :].astype(F32)
        after = jnp.minimum(b + 1, blocks - 1)
        later = ref[pl.ds(pl.multiple_of(after * BLOCK, BLOCK), BLOCK), :].astype(F32)
        later = jnp.where(b + 1 < blocks, later, 0.0)
        row = jnp.where(is_last, here, later)
        pair = [jnp.where(is_first_head, row, 0.0), jnp.where(is_first_head, 0.0, row)]
        return jnp.concatenate(pair, axis=0).astype(BF16)

    def both(wide):
        return jnp.where(is_first_head, wide[:BLOCK], wide[BLOCK:])

    def step(b, carry):
        last_out, last_grad = carry
        first, second = slots[0, b], slots[1, b]
        query, grad = moved(queries, b), moved(grads, b)
        wide_q[b] = query
        wide_g[b] = grad
        keys = jnp.concatenate([received[first, 0], received[second, 0]], axis=0)
        values = jnp.concatenate([received[first, 1], received[second, 1]], axis=0)
        scores = lax.dot_general(query, keys, NT, preferred_element_type=F32) * scale
        weights = jnp.exp(scores - jnp.max(scores, axis=-1, keepdims=True))
        probs = weights * (1.0 / jnp.sum(weights, axis=-1, keepdims=True))
        probs_low = probs.astype(BF16)
        new_out = both(jnp.dot(probs_low, values, preferred_element_type=F32))
        grad_probs = lax.dot_general(grad, values, NT, preferred_element_type=F32)
        inner = jnp.sum(probs * grad_probs, axis=-1, keepdims=True)
        grad_scores = (probs * (grad_probs - inner) * scale).astype(BF16)
        new_grad = both(jnp.dot(grad_scores, keys, preferred_element_type=F32))
        for n in range(2):
            probs_kept[n * blocks + b] = probs_low[:, n * NBLEN : (n + 1) * NBLEN]
            scores_kept[n * blocks + b] = grad_scores[:, n * NBLEN : (n + 1) * NBLEN]
        here = pl.ds(pl.multiple_of(b * BLOCK, BLOCK), BLOCK)
        out[here, :] = jnp.where(is_last, new_out, last_out).astype(BF16)
        query_grads[here, :] = jnp.where(is_last, new_grad, last_grad).astype(BF16)
        return new_out, new_grad

    zeros = jnp.zeros((BLOCK, PAIR), F32)
    lax.fori_loop(0, blocks, step, (zeros, zeros), unroll=2)


def slot_pass(slots, ranks, wide_q, wide_g, probs_kept, scores_kept, running, sums, slot_grads):
    neighbours, blocks = slots.shape
    sums[...] = jnp.zeros_like(sums)

    def step(u, before):
        use = ranks[0, u]
        neighbour = lax.div(use, blocks)
        block = use - neighbour * blocks
        slot = slots[neighbour, block]
        for part, (kept, wide) in enumerate(((scores_kept, wide_q), (probs_kept, wide_g))):
            new = lax.dot_general(kept[use], wide[block], TN, preferred_element_type=F32)
            new = jnp.where(slot != before, 0.0, sums[part]) + new
            sums[part] = new
            running[u, part] = new.astype(BF16)
        return slot

    def pick(s, carry):
        slot_grads[s] = running[ranks[1, s]]
        return carry

    lax.fori_loop(0, neighbours * blocks, step, -1, unroll=2)
    lax.fori_loop(0, slot_grads.shape[0], pick, 0)


def everything_kernel(
    enc_count, seq_count, chunks,
    entries, slots, queries, grads, pool, context, grad_queries, returned,
    *scratch,
):
    take = iter(scratch)
    per_chunk = [[next(take) for _ in range(8)] for _ in range(chunks)]
    wide_q, wide_g, probs_kept, scores_kept, running, sums = [next(take) for _ in range(6)]
    rank_ref, ranks, pool_sems, send_sems, recv_sems, rank_sem = [next(take) for _ in range(6)]

    enc_here, seq_here = lax.axis_index("enc"), lax.axis_index("seq")
    rows = queries.shape[0]
    width = pool.shape[-1]
    mine = pl.ds(pl.multiple_of(seq_here * rows, rows), rows)

    def peer_of(here, k, count):
        return lax.rem(here + k, count)

    loads = []
    for c in range(chunks):
        own = per_chunk[c][0]
        loads.append(pltpu.make_async_copy(pool.at[:, :, :, pl.ds(c * PAIR, PAIR)], own, pool_sems.at[c]))
        loads[-1].start()

    barrier = pltpu.get_barrier_semaphore()

    def greet_enc(k, carry):
        pl.semaphore_signal(
            barrier, inc=1, device_id={"enc": peer_of(enc_here, k, enc_count)}, device_id_type=MESH
        )
        return carry

    def greet_seq(k, carry):
        pl.semaphore_signal(
            barrier, inc=1, device_id={"seq": peer_of(seq_here, k, seq_count)}, device_id_type=MESH
        )
        return carry

    lax.fori_loop(1, enc_count, greet_enc, 0)
    lax.fori_loop(1, seq_count, greet_seq, 0)

    def pick(c):
        loads[c].wait()
        own, outgoing = per_chunk[c][0], per_chunk[c][1]

        def body(e, carry):
            outgoing[e] = own[entries[e]]
            return carry

        lax.fori_loop(0, enc_count, body, 0)

    def exchange(group, axis, here, count, source_of, target_of):
        def body(k, carry):
            peer = peer_of(here, k, count)
            pltpu.make_async_remote_copy(
                src_ref=source_of(peer),
                dst_ref=target_of(here),
                send_sem=send_sems.at[group],
                recv_sem=recv_sems.at[group],
                device_id={axis: peer},
                device_id_type=MESH,
            ).start()
            return carry

        lax.fori_loop(1, count, body, 0)
        pltpu.make_async_copy(source_of(here), target_of(here), recv_sems.at[group]).start()

    def cut(c, p):
        return pl.ds(pl.multiple_of(p * width + c * PAIR, PAIR), PAIR)

    def token_rows(p):
        return pl.ds(pl.multiple_of(p * rows, rows), rows)

    def fetch(c):
        own, outgoing, arrived = per_chunk[c][:3]
        exchange(6 * c, "enc", enc_here, enc_count, lambda p: outgoing.at[p], lambda p: arrived.at[p])

    def to_heads(c):
        head_queries, head_grads = per_chunk[c][3:5]
        for n, (source, target) in enumerate(((queries, head_queries), (grads, head_grads))):
            exchange(
                6 * c + 1 + n, "seq", seq_here, seq_count,
                lambda p, source=source: source.at[:, cut(c, p)],
                lambda p, target=target: target.at[token_rows(p), :],
            )

    def to_tokens(c):
        out, query_grads = per_chunk[c][5:7]
        for n, (source, target) in enumerate(((out, context), (query_grads, grad_queries))):
            exchange(
                6 * c + 3 + n, "seq", seq_here, seq_count,
                lambda p, source=source: source.at[token_rows(p), :],
                lambda p, target=target: target.at[:, cut(c, p)],
            )

    def give_back(c):
        slot_grads = per_chunk[c][7]
        exchange(
            6 * c + 5, "enc", enc_here, enc_count,
            lambda p: slot_grads.at[p], lambda p: returned.at[c, p],
        )

    def whole(ref, sem):
        pltpu.make_async_copy(ref, ref, sem).wait()

    def sent(group, ref, count):
        part = ref.at[pl.ds(0, ref.shape[0] // count * (count - 1))]
        whole(part, send_sems.at[group])

    def arrive(group, ref):
        whole(ref, recv_sems.at[group])

    def compute(c):
        _, _, arrived, head_queries, head_grads, out, query_grads, slot_grads = per_chunk[c]
        arrive(6 * c, arrived)
        arrive(6 * c + 1, head_queries)
        arrive(6 * c + 2, head_grads)
        block_pass(
            slots, head_queries, head_grads, arrived, out, query_grads,
            wide_q, wide_g, probs_kept, scores_kept,
        )
        to_tokens(c)
        slot_pass(
            slots, ranks, wide_q, wide_g, probs_kept, scores_kept, running, sums, slot_grads
        )

    pick(0)
    pl.semaphore_wait(barrier, enc_count + seq_count - 2)
    fetch(0)
    to_heads(0)
    for c in range(1, chunks):
        pick(c)
    sort_uses(slots, rank_ref, ranks, rank_sem.at[0])
    for c in range(chunks):
        sent(6 * c, per_chunk[c][1], enc_count)
        if c + 1 < chunks:
            fetch(c + 1)
            to_heads(c + 1)
        if c > 0:
            give_back(c - 1)
        compute(c)
    give_back(chunks - 1)

    for c in range(chunks):
        _, _, arrived, head_queries, head_grads, out, query_grads, slot_grads = per_chunk[c]
        sent(6 * c + 1, head_queries, seq_count)
        sent(6 * c + 2, head_grads, seq_count)
        sent(6 * c + 3, out, seq_count)
        sent(6 * c + 4, query_grads, seq_count)
        sent(6 * c + 5, slot_grads, enc_count)
        arrive(6 * c + 3, out)
        arrive(6 * c + 4, query_grads)
        arrive(6 * c + 5, slot_grads)


def everything(enc_count, seq_count, entries, slots, queries, grads, pool):
    rows = queries.shape[0]
    held, _, _, width = pool.shape
    chunks = width // PAIR
    length = rows * seq_count
    blocks = length // BLOCK
    tokens = jax.ShapeDtypeStruct(queries.shape, queries.dtype)

    def entry_buffer(count):
        return pltpu.VMEM((count, 2, NBLEN, PAIR), BF16)

    heads = pltpu.VMEM((length, PAIR), BF16)
    chunk_shapes = [
        entry_buffer(held), entry_buffer(enc_count), entry_buffer(enc_count),
        heads, heads, heads, heads, entry_buffer(enc_count),
    ]
    return pl.pallas_call(
        functools.partial(everything_kernel, enc_count, seq_count, chunks),
        out_shape=(
            tokens,
            tokens,
            jax.ShapeDtypeStruct((chunks, enc_count, 2, NBLEN, PAIR), pool.dtype),
        ),
        in_specs=[SCALAR] * 2 + [ANY] * 3,
        out_specs=(ANY, ANY, ANY),
        scratch_shapes=chunk_shapes * chunks
        + [
            pltpu.VMEM((blocks, 2 * BLOCK, PAIR), BF16),
            pltpu.VMEM((blocks, 2 * BLOCK, PAIR), BF16),
            pltpu.VMEM((2 * blocks, 2 * BLOCK, NBLEN), BF16),
            pltpu.VMEM((2 * blocks, 2 * BLOCK, NBLEN), BF16),
            pltpu.VMEM((2 * blocks, 2, NBLEN, PAIR), BF16),
            pltpu.VMEM((2, NBLEN, PAIR), F32),
            pltpu.VMEM((8, 128), jnp.int32),
            pltpu.SMEM((8, 128), jnp.int32),
            pltpu.SemaphoreType.DMA((chunks,)),
            pltpu.SemaphoreType.DMA((6 * chunks,)),
            pltpu.SemaphoreType.DMA((6 * chunks,)),
            pltpu.SemaphoreType.DMA((1,)),
        ],
        compiler_params=pltpu.CompilerParams(
            collective_id=0, has_side_effects=True, vmem_limit_bytes=56 * MIB
        ),
    )(entries, slots, queries, grads, pool)


def owner_kernel(entries, returned, context, grad_queries, pool_grads, context_out, grad_out, total):
    context_out[...] = context[...]
    grad_out[...] = grad_queries[...]
    total[...] = jnp.zeros_like(total)

    def step(e, carry):
        total[entries[e]] += returned[e].astype(F32)
        return carry

    lax.fori_loop(0, returned.shape[0], step, 0)
    pool_grads[...] = total[...].astype(pool_grads.dtype)


def owner_sum(entries, returned, context, grad_queries, pool_shape):
    cuts = 2
    chunks, count, two, length, width = returned.shape
    part = length // cuts
    rows, columns = context.shape
    tokens = jax.ShapeDtypeStruct(context.shape, context.dtype)
    token_block = pl.BlockSpec((rows, columns // (chunks * cuts)), lambda c, i: (0, c * cuts + i))
    return pl.pallas_call(
        owner_kernel,
        out_shape=(jax.ShapeDtypeStruct(pool_shape, returned.dtype), tokens, tokens),
        grid=(chunks, cuts),
        in_specs=[
            SCALAR,
            pl.BlockSpec((None, count, two, part, width), lambda c, i: (c, 0, 0, i, 0)),
            token_block,
            token_block,
        ],
        out_specs=(
            pl.BlockSpec((pool_shape[0], two, part, width), lambda c, i: (0, 0, i, c)),
            token_block,
            token_block,
        ),
        scratch_shapes=[pltpu.VMEM((pool_shape[0], two, part, width), F32)],
        compiler_params=pltpu.CompilerParams(vmem_limit_bytes=58 * MIB),
    )(entries, returned, context, grad_queries)


def local(enc_count, seq_count, queries, kv_pool, send_lists, block_slots, grad_context):
    entries = send_lists.reshape(-1)
    slots = block_slots[0].T
    context, grad_queries, returned = everything(
        enc_count, seq_count, entries, slots, queries[0], grad_context[0], kv_pool
    )
    pool_grads, context, grad_queries = owner_sum(
        entries, returned, context, grad_queries, kv_pool.shape
    )
    return context[None], grad_queries[None], pool_grads


def solution(mesh):
    in_specs = (
        P("enc", "seq", None),
        P("enc", None, None, "seq"),
        P("enc", None, None),
        P("enc", None, None),
        P("enc", "seq", None),
    )
    out_specs = (P("enc", "seq", None), P("enc", "seq", None), P("enc", None, None, "seq"))
    body = functools.partial(local, mesh.shape["enc"], mesh.shape["seq"])
    return jax.shard_map(body, mesh=mesh, in_specs=in_specs, out_specs=out_specs, check_vma=False)
```

```python
import functools

import jax
import jax.numpy as jnp
from jax import lax
from jax.experimental import pallas as pl
from jax.experimental.pallas import tpu as pltpu
from jax.sharding import PartitionSpec as P

DH = 128
BLOCK = 64
NBLEN = 128
PAIR = 2 * DH
MESH = pl.DeviceIdType.MESH
ANY = pl.BlockSpec(memory_space=pl.ANY)
IN_VMEM = pl.BlockSpec(memory_space=pltpu.VMEM)
SCALAR = pl.BlockSpec(memory_space=pltpu.SMEM)
MIB = 1 << 20
NT = (((1,), (1,)), ((), ()))
TN = (((0,), (0,)), ((), ()))
F32 = jnp.float32
BF16 = jnp.bfloat16


def sort_uses(slots, rank_ref, first_row):
    neighbours, blocks = slots.shape
    uses = neighbours * blocks
    lane = lax.broadcasted_iota(jnp.int32, (uses, 128), 1)
    row = lax.broadcasted_iota(jnp.int32, (uses, 128), 0)
    along_lanes = jnp.full((uses, 128), uses * 128, jnp.int32)
    along_rows = jnp.zeros((uses, 128), jnp.int32)
    slot_rows = jnp.zeros((uses, 128), jnp.int32)
    for n in range(neighbours):

        def put(b, carry, n=n):
            along_lanes, along_rows, slot_rows = carry
            use = n * blocks + b
            key = slots[n, b] * uses + use
            along_lanes = jnp.where(lane == use, key, along_lanes)
            along_rows = jnp.where(row == use, key, along_rows)
            slot_rows = jnp.where(row == use, slots[n, b], slot_rows)
            return along_lanes, along_rows, slot_rows

        along_lanes, along_rows, slot_rows = lax.fori_loop(
            0, blocks, put, (along_lanes, along_rows, slot_rows)
        )
    rank = jnp.sum((along_lanes < along_rows).astype(jnp.int32), axis=1, keepdims=True)
    order = jnp.sum(jnp.where(rank == lane, row, 0), axis=0, keepdims=True)
    ends = jnp.sum((slot_rows <= lane).astype(jnp.int32), axis=0, keepdims=True) - 1
    rank_ref[first_row : first_row + 1, :] = order
    rank_ref[first_row + 1 : first_row + 2, :] = ends


def block_pass(slots, queries, grads, received, out, query_grads, wide_q, wide_g, probs_kept, scores_kept):
    blocks = queries.shape[0] // BLOCK
    scale = DH ** (-0.5)
    is_last = lax.broadcasted_iota(jnp.int32, (BLOCK, PAIR), 0) == BLOCK - 1
    is_first_head = lax.broadcasted_iota(jnp.int32, (BLOCK, PAIR), 1) < DH

    def moved(ref, b):
        here = ref[pl.ds(pl.multiple_of(b * BLOCK, BLOCK), BLOCK), :].astype(F32)
        after = jnp.minimum(b + 1, blocks - 1)
        later = ref[pl.ds(pl.multiple_of(after * BLOCK, BLOCK), BLOCK), :].astype(F32)
        later = jnp.where(b + 1 < blocks, later, 0.0)
        row = jnp.where(is_last, here, later)
        pair = [jnp.where(is_first_head, row, 0.0), jnp.where(is_first_head, 0.0, row)]
        return jnp.concatenate(pair, axis=0).astype(BF16)

    def both(wide):
        return jnp.where(is_first_head, wide[:BLOCK], wide[BLOCK:])

    def step(b, carry):
        last_out, last_grad = carry
        first, second = slots[0, b], slots[1, b]
        query, grad = moved(queries, b), moved(grads, b)
        wide_q[b] = query
        wide_g[b] = grad
        keys = jnp.concatenate([received[first, 0], received[second, 0]], axis=0)
        values = jnp.concatenate([received[first, 1], received[second, 1]], axis=0)
        scores = lax.dot_general(query, keys, NT, preferred_element_type=F32) * scale
        weights = jnp.exp(scores - jnp.max(scores, axis=-1, keepdims=True))
        probs = weights * (1.0 / jnp.sum(weights, axis=-1, keepdims=True))
        probs_low = probs.astype(BF16)
        new_out = both(jnp.dot(probs_low, values, preferred_element_type=F32))
        grad_probs = lax.dot_general(grad, values, NT, preferred_element_type=F32)
        inner = jnp.sum(probs * grad_probs, axis=-1, keepdims=True)
        grad_scores = (probs * (grad_probs - inner) * scale).astype(BF16)
        new_grad = both(jnp.dot(grad_scores, keys, preferred_element_type=F32))
        for n in range(2):
            probs_kept[n * blocks + b] = probs_low[:, n * NBLEN : (n + 1) * NBLEN]
            scores_kept[n * blocks + b] = grad_scores[:, n * NBLEN : (n + 1) * NBLEN]
        here = pl.ds(pl.multiple_of(b * BLOCK, BLOCK), BLOCK)
        out[here, :] = jnp.where(is_last, new_out, last_out).astype(BF16)
        query_grads[here, :] = jnp.where(is_last, new_grad, last_grad).astype(BF16)
        return new_out, new_grad

    zeros = jnp.zeros((BLOCK, PAIR), F32)
    lax.fori_loop(0, blocks, step, (zeros, zeros), unroll=2)


def slot_pass(slots, ranks, wide_q, wide_g, probs_kept, scores_kept, running, sums, slot_grads):
    neighbours, blocks = slots.shape
    sums[...] = jnp.zeros_like(sums)

    def step(u, before):
        use = ranks[0, u]
        neighbour = lax.div(use, blocks)
        block = use - neighbour * blocks
        slot = slots[neighbour, block]
        for part, (kept, wide) in enumerate(((scores_kept, wide_q), (probs_kept, wide_g))):
            new = lax.dot_general(kept[use], wide[block], TN, preferred_element_type=F32)
            new = jnp.where(slot != before, 0.0, sums[part]) + new
            sums[part] = new
            running[u, part] = new.astype(BF16)
        return slot

    def pick(s, carry):
        slot_grads[s] = running[ranks[1, s]]
        return carry

    lax.fori_loop(0, neighbours * blocks, step, -1, unroll=2)
    lax.fori_loop(0, slot_grads.shape[0], pick, 0)


def owner_pass(entries, ranks, returned, running, sums, store):
    def step(place, before):
        sender = ranks[2, place]
        entry = entries[0, sender]
        for part in range(2):
            new = returned[sender, part].astype(F32)
            new = jnp.where(entry != before, 0.0, sums[part]) + new
            sums[part] = new
            running[place, part] = new.astype(BF16)
        return entry

    sums[...] = jnp.zeros_like(sums)
    lax.fori_loop(0, entries.shape[1], step, -1)
    store(lambda entry: running[ranks[3, entry]])


def everything_kernel(
    enc_count, seq_count, chunks,
    entries, slots, queries, grads, pool, context, grad_queries, pool_grads,
    *scratch,
):
    take = iter(scratch)
    per_chunk = [[next(take) for _ in range(9)] for _ in range(chunks)]
    wide_q, wide_g, probs_kept, scores_kept, running, sums = [next(take) for _ in range(6)]
    rank_ref, ranks, pool_sems, send_sems, recv_sems, rank_sem = [next(take) for _ in range(6)]

    enc_here, seq_here = lax.axis_index("enc"), lax.axis_index("seq")
    rows = queries.shape[0]
    width = pool.shape[-1]
    mine = pl.ds(pl.multiple_of(seq_here * rows, rows), rows)

    def peer_of(here, k, count):
        return lax.rem(here + k, count)

    loads = []
    for c in range(chunks):
        own = per_chunk[c][0]
        loads.append(pltpu.make_async_copy(pool.at[:, :, :, pl.ds(c * PAIR, PAIR)], own, pool_sems.at[c]))
        loads[-1].start()

    barrier = pltpu.get_barrier_semaphore()

    def greet_enc(k, carry):
        pl.semaphore_signal(
            barrier, inc=1, device_id={"enc": peer_of(enc_here, k, enc_count)}, device_id_type=MESH
        )
        return carry

    def greet_seq(k, carry):
        pl.semaphore_signal(
            barrier, inc=1, device_id={"seq": peer_of(seq_here, k, seq_count)}, device_id_type=MESH
        )
        return carry

    lax.fori_loop(1, enc_count, greet_enc, 0)
    lax.fori_loop(1, seq_count, greet_seq, 0)

    def pick(c):
        loads[c].wait()
        own, outgoing = per_chunk[c][0], per_chunk[c][1]

        def body(e, carry):
            outgoing[e] = own[entries[0, e]]
            return carry

        lax.fori_loop(0, enc_count, body, 0)

    def exchange(group, axis, here, count, source_of, target_of):
        def body(i, carry):
            k = count // 2 + (1 - 2 * lax.rem(i, 2)) * lax.div(i + 1, 2)
            peer = peer_of(here, k, count)
            pltpu.make_async_remote_copy(
                src_ref=source_of(peer),
                dst_ref=target_of(here),
                send_sem=send_sems.at[group],
                recv_sem=recv_sems.at[group],
                device_id={axis: peer},
                device_id_type=MESH,
            ).start()
            return carry

        lax.fori_loop(0, count - 1, body, 0)
        pltpu.make_async_copy(source_of(here), target_of(here), recv_sems.at[group]).start()

    def cut(c, p):
        return pl.ds(pl.multiple_of(p * width + c * PAIR, PAIR), PAIR)

    def token_rows(p):
        return pl.ds(pl.multiple_of(p * rows, rows), rows)

    def fetch(c):
        own, outgoing, arrived = per_chunk[c][:3]
        exchange(6 * c, "enc", enc_here, enc_count, lambda p: outgoing.at[p], lambda p: arrived.at[p])

    def to_heads(c):
        head_queries, head_grads = per_chunk[c][3:5]
        for n, (source, target) in enumerate(((queries, head_queries), (grads, head_grads))):
            exchange(
                6 * c + 1 + n, "seq", seq_here, seq_count,
                lambda p, source=source: source.at[:, cut(c, p)],
                lambda p, target=target: target.at[token_rows(p), :],
            )

    def to_tokens(c):
        out, query_grads = per_chunk[c][5:7]
        for n, (source, target) in enumerate(((out, context), (query_grads, grad_queries))):
            exchange(
                6 * c + 3 + n, "seq", seq_here, seq_count,
                lambda p, source=source: source.at[token_rows(p), :],
                lambda p, target=target: target.at[:, cut(c, p)],
            )

    def give_back(c):
        slot_grads, returned = per_chunk[c][7:9]
        exchange(
            6 * c + 5, "enc", enc_here, enc_count,
            lambda p: slot_grads.at[p], lambda p: returned.at[p],
        )

    def whole(ref, sem):
        pltpu.make_async_copy(ref, ref, sem).wait()

    def sent(group, ref, count):
        part = ref.at[pl.ds(0, ref.shape[0] // count * (count - 1))]
        whole(part, send_sems.at[group])

    def arrive(group, ref):
        whole(ref, recv_sems.at[group])

    def compute(c):
        _, _, arrived, head_queries, head_grads, out, query_grads, slot_grads, returned = per_chunk[c]
        arrive(6 * c, arrived)
        arrive(6 * c + 1, head_queries)
        arrive(6 * c + 2, head_grads)
        block_pass(
            slots, head_queries, head_grads, arrived, out, query_grads,
            wide_q, wide_g, probs_kept, scores_kept,
        )
        to_tokens(c)
        slot_pass(
            slots, ranks, wide_q, wide_g, probs_kept, scores_kept, running, sums, slot_grads
        )

    pick(0)
    pl.semaphore_wait(barrier, enc_count + seq_count - 2)
    fetch(0)
    to_heads(0)
    for c in range(1, chunks):
        pick(c)
    sort_uses(slots, rank_ref, 0)
    sort_uses(entries, rank_ref, 2)
    copy = pltpu.make_async_copy(rank_ref, ranks, rank_sem.at[0])
    copy.start()
    copy.wait()
    for c in range(chunks):
        sent(6 * c, per_chunk[c][1], enc_count)
        if c + 1 < chunks:
            fetch(c + 1)
            to_heads(c + 1)
        if c > 0:
            give_back(c - 1)
        compute(c)
    give_back(chunks - 1)

    for c in range(chunks):
        _, _, arrived, head_queries, head_grads, out, query_grads, slot_grads, returned = per_chunk[c]
        sent(6 * c + 1, head_queries, seq_count)
        sent(6 * c + 2, head_grads, seq_count)
        sent(6 * c + 3, out, seq_count)
        sent(6 * c + 4, query_grads, seq_count)
        sent(6 * c + 5, slot_grads, enc_count)
        arrive(6 * c + 3, out)
        arrive(6 * c + 4, query_grads)
        arrive(6 * c + 5, returned)

        def store(value, c=c):
            def body(entry, carry):
                pool_grads[entry, :, :, c * PAIR : (c + 1) * PAIR] = value(entry)
                return carry

            lax.fori_loop(0, pool_grads.shape[0], body, 0)

        owner_pass(entries, ranks, returned, running, sums, store)


def everything(enc_count, seq_count, entries, slots, queries, grads, pool):
    rows = queries.shape[0]
    held, _, _, width = pool.shape
    chunks = width // PAIR
    length = rows * seq_count
    blocks = length // BLOCK
    tokens = pltpu.VMEM(queries.shape, queries.dtype)

    def entry_buffer(count):
        return pltpu.VMEM((count, 2, NBLEN, PAIR), BF16)

    heads = pltpu.VMEM((length, PAIR), BF16)
    chunk_shapes = [
        entry_buffer(held), entry_buffer(enc_count), entry_buffer(enc_count),
        heads, heads, heads, heads, entry_buffer(enc_count), entry_buffer(enc_count),
    ]
    return pl.pallas_call(
        functools.partial(everything_kernel, enc_count, seq_count, chunks),
        out_shape=(
            tokens,
            tokens,
            pltpu.VMEM(pool.shape, pool.dtype),
        ),
        in_specs=[SCALAR] * 2 + [ANY] * 3,
        out_specs=(ANY, ANY, IN_VMEM),
        scratch_shapes=chunk_shapes * chunks
        + [
            pltpu.VMEM((blocks, 2 * BLOCK, PAIR), BF16),
            pltpu.VMEM((blocks, 2 * BLOCK, PAIR), BF16),
            pltpu.VMEM((2 * blocks, 2 * BLOCK, NBLEN), BF16),
            pltpu.VMEM((2 * blocks, 2 * BLOCK, NBLEN), BF16),
            pltpu.VMEM((2 * blocks, 2, NBLEN, PAIR), BF16),
            pltpu.VMEM((2, NBLEN, PAIR), F32),
            pltpu.VMEM((8, 128), jnp.int32),
            pltpu.SMEM((8, 128), jnp.int32),
            pltpu.SemaphoreType.DMA((chunks,)),
            pltpu.SemaphoreType.DMA((6 * chunks,)),
            pltpu.SemaphoreType.DMA((6 * chunks,)),
            pltpu.SemaphoreType.DMA((1,)),
        ],
        compiler_params=pltpu.CompilerParams(
            collective_id=0, has_side_effects=True, vmem_limit_bytes=54 * MIB
        ),
    )(entries, slots, queries, grads, pool)


def local(enc_count, seq_count, queries, kv_pool, send_lists, block_slots, grad_context):
    entries = send_lists.reshape(1, -1)
    slots = block_slots[0].T
    context, grad_queries, pool_grads = everything(
        enc_count, seq_count, entries, slots, queries[0], grad_context[0], kv_pool
    )
    return context[None], grad_queries[None], pool_grads


def solution(mesh):
    in_specs = (
        P("enc", "seq", None),
        P("enc", None, None, "seq"),
        P("enc", None, None),
        P("enc", None, None),
        P("enc", "seq", None),
    )
    out_specs = (P("enc", "seq", None), P("enc", "seq", None), P("enc", None, None, "seq"))
    body = functools.partial(local, mesh.shape["enc"], mesh.shape["seq"])
    return jax.shard_map(body, mesh=mesh, in_specs=in_specs, out_specs=out_specs, check_vma=False)
```

```python
import functools

import jax
import jax.numpy as jnp
from jax import lax
from jax.experimental import pallas as pl
from jax.experimental.pallas import tpu as pltpu
from jax.sharding import PartitionSpec as P

DH = 128
BLOCK = 64
NBLEN = 128
PAIR = 2 * DH
MESH = pl.DeviceIdType.MESH
ANY = pl.BlockSpec(memory_space=pl.ANY)
IN_VMEM = pl.BlockSpec(memory_space=pltpu.VMEM)
SCALAR = pl.BlockSpec(memory_space=pltpu.SMEM)
MIB = 1 << 20
NT = (((1,), (1,)), ((), ()))
TN = (((0,), (0,)), ((), ()))
F32 = jnp.float32
BF16 = jnp.bfloat16


def sort_uses(slots, rank_ref, first_row):
    neighbours, blocks = slots.shape
    uses = neighbours * blocks
    lane = lax.broadcasted_iota(jnp.int32, (uses, 128), 1)
    row = lax.broadcasted_iota(jnp.int32, (uses, 128), 0)
    along_lanes = jnp.full((uses, 128), uses * 128, jnp.int32)
    along_rows = jnp.zeros((uses, 128), jnp.int32)
    slot_rows = jnp.zeros((uses, 128), jnp.int32)
    for n in range(neighbours):

        def put(b, carry, n=n):
            along_lanes, along_rows, slot_rows = carry
            use = n * blocks + b
            key = slots[n, b] * uses + use
            along_lanes = jnp.where(lane == use, key, along_lanes)
            along_rows = jnp.where(row == use, key, along_rows)
            slot_rows = jnp.where(row == use, slots[n, b], slot_rows)
            return along_lanes, along_rows, slot_rows

        along_lanes, along_rows, slot_rows = lax.fori_loop(
            0, blocks, put, (along_lanes, along_rows, slot_rows)
        )
    rank = jnp.sum((along_lanes < along_rows).astype(jnp.int32), axis=1, keepdims=True)
    order = jnp.sum(jnp.where(rank == lane, row, 0), axis=0, keepdims=True)
    ends = jnp.sum((slot_rows <= lane).astype(jnp.int32), axis=0, keepdims=True) - 1
    rank_ref[first_row : first_row + 1, :] = order
    rank_ref[first_row + 1 : first_row + 2, :] = ends


def block_pass(slots, queries, grads, received, out, query_grads, wide_q, wide_g, probs_kept, scores_kept):
    blocks = queries.shape[0] // BLOCK
    scale = DH ** (-0.5)
    is_last = lax.broadcasted_iota(jnp.int32, (BLOCK, PAIR), 0) == BLOCK - 1
    is_first_head = lax.broadcasted_iota(jnp.int32, (BLOCK, PAIR), 1) < DH

    def moved(ref, b):
        here = ref[pl.ds(pl.multiple_of(b * BLOCK, BLOCK), BLOCK), :].astype(F32)
        after = jnp.minimum(b + 1, blocks - 1)
        later = ref[pl.ds(pl.multiple_of(after * BLOCK, BLOCK), BLOCK), :].astype(F32)
        later = jnp.where(b + 1 < blocks, later, 0.0)
        row = jnp.where(is_last, here, later)
        pair = [jnp.where(is_first_head, row, 0.0), jnp.where(is_first_head, 0.0, row)]
        return jnp.concatenate(pair, axis=0).astype(BF16)

    def both(wide):
        return jnp.where(is_first_head, wide[:BLOCK], wide[BLOCK:])

    def step(b, carry):
        last_out, last_grad = carry
        first, second = slots[0, b], slots[1, b]
        query, grad = moved(queries, b), moved(grads, b)
        wide_q[b] = query
        wide_g[b] = grad
        keys = jnp.concatenate([received[first, 0], received[second, 0]], axis=0)
        values = jnp.concatenate([received[first, 1], received[second, 1]], axis=0)
        scores = lax.dot_general(query, keys, NT, preferred_element_type=F32) * scale
        weights = jnp.exp(scores - jnp.max(scores, axis=-1, keepdims=True))
        probs = weights * (1.0 / jnp.sum(weights, axis=-1, keepdims=True))
        probs_low = probs.astype(BF16)
        new_out = both(jnp.dot(probs_low, values, preferred_element_type=F32))
        grad_probs = lax.dot_general(grad, values, NT, preferred_element_type=F32)
        inner = jnp.sum(probs * grad_probs, axis=-1, keepdims=True)
        grad_scores = (probs * (grad_probs - inner) * scale).astype(BF16)
        new_grad = both(jnp.dot(grad_scores, keys, preferred_element_type=F32))
        for n in range(2):
            probs_kept[n * blocks + b] = probs_low[:, n * NBLEN : (n + 1) * NBLEN]
            scores_kept[n * blocks + b] = grad_scores[:, n * NBLEN : (n + 1) * NBLEN]
        here = pl.ds(pl.multiple_of(b * BLOCK, BLOCK), BLOCK)
        out[here, :] = jnp.where(is_last, new_out, last_out).astype(BF16)
        query_grads[here, :] = jnp.where(is_last, new_grad, last_grad).astype(BF16)
        return new_out, new_grad

    zeros = jnp.zeros((BLOCK, PAIR), F32)
    lax.fori_loop(0, blocks, step, (zeros, zeros), unroll=2)


def slot_pass(slots, ranks, wide_q, wide_g, probs_kept, scores_kept, running, sums, slot_grads):
    neighbours, blocks = slots.shape
    sums[...] = jnp.zeros_like(sums)

    def step(u, before):
        use = ranks[0, u]
        neighbour = lax.div(use, blocks)
        block = use - neighbour * blocks
        slot = slots[neighbour, block]
        for part, (kept, wide) in enumerate(((scores_kept, wide_q), (probs_kept, wide_g))):
            new = lax.dot_general(kept[use], wide[block], TN, preferred_element_type=F32)
            new = jnp.where(slot != before, 0.0, sums[part]) + new
            sums[part] = new
            running[u, part] = new.astype(BF16)
        return slot

    def pick(s, carry):
        slot_grads[s] = running[ranks[1, s]]
        return carry

    lax.fori_loop(0, neighbours * blocks, step, -1, unroll=2)
    lax.fori_loop(0, slot_grads.shape[0], pick, 0)


def owner_pass(entries, ranks, returned, running, sums, store):
    def step(place, before):
        sender = ranks[2, place]
        entry = entries[0, sender]
        for part in range(2):
            new = returned[sender, part].astype(F32)
            new = jnp.where(entry != before, 0.0, sums[part]) + new
            sums[part] = new
            running[place, part] = new.astype(BF16)
        return entry

    sums[...] = jnp.zeros_like(sums)
    lax.fori_loop(0, entries.shape[1], step, -1)
    store(lambda entry: running[ranks[3, entry]])


def everything_kernel(
    enc_count, seq_count, chunks,
    entries, slots, queries, grads, pool, context, grad_queries, early_sums, last_returned,
    *scratch,
):
    take = iter(scratch)
    per_chunk = [[next(take) for _ in range(9)] for _ in range(chunks - 1)]
    per_chunk.append([next(take) for _ in range(8)] + [last_returned])
    wide_q, wide_g, probs_kept, scores_kept, running, sums = [next(take) for _ in range(6)]
    rank_ref, ranks, pool_sems, send_sems, recv_sems, rank_sem = [next(take) for _ in range(6)]

    enc_here, seq_here = lax.axis_index("enc"), lax.axis_index("seq")
    rows = queries.shape[0]
    width = pool.shape[-1]
    mine = pl.ds(pl.multiple_of(seq_here * rows, rows), rows)

    def peer_of(here, k, count):
        return lax.rem(here + k, count)

    loads = []
    for c in range(chunks):
        own = per_chunk[c][0]
        loads.append(pltpu.make_async_copy(pool.at[:, :, :, pl.ds(c * PAIR, PAIR)], own, pool_sems.at[c]))
        loads[-1].start()

    barrier = pltpu.get_barrier_semaphore()

    def greet_enc(k, carry):
        pl.semaphore_signal(
            barrier, inc=1, device_id={"enc": peer_of(enc_here, k, enc_count)}, device_id_type=MESH
        )
        return carry

    def greet_seq(k, carry):
        pl.semaphore_signal(
            barrier, inc=1, device_id={"seq": peer_of(seq_here, k, seq_count)}, device_id_type=MESH
        )
        return carry

    lax.fori_loop(1, enc_count, greet_enc, 0)
    lax.fori_loop(1, seq_count, greet_seq, 0)

    def pick(c):
        loads[c].wait()
        own, outgoing = per_chunk[c][0], per_chunk[c][1]

        def body(e, carry):
            outgoing[e] = own[entries[0, e]]
            return carry

        lax.fori_loop(0, enc_count, body, 0)

    def exchange(group, axis, here, count, source_of, target_of):
        def body(i, carry):
            k = count // 2 + (1 - 2 * lax.rem(i, 2)) * lax.div(i + 1, 2)
            peer = peer_of(here, k, count)
            pltpu.make_async_remote_copy(
                src_ref=source_of(peer),
                dst_ref=target_of(here),
                send_sem=send_sems.at[group],
                recv_sem=recv_sems.at[group],
                device_id={axis: peer},
                device_id_type=MESH,
            ).start()
            return carry

        lax.fori_loop(0, count - 1, body, 0)
        pltpu.make_async_copy(source_of(here), target_of(here), recv_sems.at[group]).start()

    def cut(c, p):
        return pl.ds(pl.multiple_of(p * width + c * PAIR, PAIR), PAIR)

    def token_rows(p):
        return pl.ds(pl.multiple_of(p * rows, rows), rows)

    def fetch(c):
        own, outgoing, arrived = per_chunk[c][:3]
        exchange(6 * c, "enc", enc_here, enc_count, lambda p: outgoing.at[p], lambda p: arrived.at[p])

    def to_heads(c):
        head_queries, head_grads = per_chunk[c][3:5]
        for n, (source, target) in enumerate(((queries, head_queries), (grads, head_grads))):
            exchange(
                6 * c + 1 + n, "seq", seq_here, seq_count,
                lambda p, source=source: source.at[:, cut(c, p)],
                lambda p, target=target: target.at[token_rows(p), :],
            )

    def to_tokens(c):
        out, query_grads = per_chunk[c][5:7]
        for n, (source, target) in enumerate(((out, context), (query_grads, grad_queries))):
            exchange(
                6 * c + 3 + n, "seq", seq_here, seq_count,
                lambda p, source=source: source.at[token_rows(p), :],
                lambda p, target=target: target.at[:, cut(c, p)],
            )

    def give_back(c):
        slot_grads, returned = per_chunk[c][7:9]
        exchange(
            6 * c + 5, "enc", enc_here, enc_count,
            lambda p: slot_grads.at[p], lambda p: returned.at[p],
        )

    def whole(ref, sem):
        pltpu.make_async_copy(ref, ref, sem).wait()

    def sent(group, ref, count):
        part = ref.at[pl.ds(0, ref.shape[0] // count * (count - 1))]
        whole(part, send_sems.at[group])

    def arrive(group, ref):
        whole(ref, recv_sems.at[group])

    def compute(c):
        _, _, arrived, head_queries, head_grads, out, query_grads, slot_grads, returned = per_chunk[c]
        arrive(6 * c, arrived)
        arrive(6 * c + 1, head_queries)
        arrive(6 * c + 2, head_grads)
        block_pass(
            slots, head_queries, head_grads, arrived, out, query_grads,
            wide_q, wide_g, probs_kept, scores_kept,
        )
        to_tokens(c)
        slot_pass(
            slots, ranks, wide_q, wide_g, probs_kept, scores_kept, running, sums, slot_grads
        )

    pick(0)
    pl.semaphore_wait(barrier, enc_count + seq_count - 2)
    fetch(0)
    to_heads(0)
    for c in range(1, chunks):
        pick(c)
    sort_uses(slots, rank_ref, 0)
    sort_uses(entries, rank_ref, 2)
    copy = pltpu.make_async_copy(rank_ref, ranks, rank_sem.at[0])
    copy.start()
    copy.wait()
    for c in range(chunks):
        sent(6 * c, per_chunk[c][1], enc_count)
        if c + 1 < chunks:
            fetch(c + 1)
            to_heads(c + 1)
        if c > 0:
            give_back(c - 1)
        compute(c)
    give_back(chunks - 1)

    for c in range(chunks):
        _, _, arrived, head_queries, head_grads, out, query_grads, slot_grads, returned = per_chunk[c]
        sent(6 * c + 1, head_queries, seq_count)
        sent(6 * c + 2, head_grads, seq_count)
        sent(6 * c + 3, out, seq_count)
        sent(6 * c + 4, query_grads, seq_count)
        sent(6 * c + 5, slot_grads, enc_count)
        arrive(6 * c + 3, out)
        arrive(6 * c + 4, query_grads)
        arrive(6 * c + 5, returned)

        if c + 1 < chunks:

            def store(value, c=c):
                def body(entry, carry):
                    early_sums[c, entry] = value(entry)
                    return carry

                lax.fori_loop(0, pool.shape[0], body, 0)

            owner_pass(entries, ranks, returned, running, sums, store)


def everything(enc_count, seq_count, entries, slots, queries, grads, pool):
    rows = queries.shape[0]
    held, _, _, width = pool.shape
    chunks = width // PAIR
    length = rows * seq_count
    blocks = length // BLOCK
    tokens = pltpu.VMEM(queries.shape, queries.dtype)

    def entry_buffer(count):
        return pltpu.VMEM((count, 2, NBLEN, PAIR), BF16)

    heads = pltpu.VMEM((length, PAIR), BF16)
    chunk_shapes = [
        entry_buffer(held), entry_buffer(enc_count), entry_buffer(enc_count),
        heads, heads, heads, heads, entry_buffer(enc_count), entry_buffer(enc_count),
    ]
    return pl.pallas_call(
        functools.partial(everything_kernel, enc_count, seq_count, chunks),
        out_shape=(
            tokens,
            tokens,
            pltpu.VMEM((chunks - 1, held, 2, NBLEN, PAIR), pool.dtype),
            pltpu.VMEM((enc_count, 2, NBLEN, PAIR), pool.dtype),
        ),
        in_specs=[SCALAR] * 2 + [ANY] * 3,
        out_specs=(ANY, ANY, IN_VMEM, IN_VMEM),
        scratch_shapes=chunk_shapes * (chunks - 1)
        + chunk_shapes[:8]
        + [
            pltpu.VMEM((blocks, 2 * BLOCK, PAIR), BF16),
            pltpu.VMEM((blocks, 2 * BLOCK, PAIR), BF16),
            pltpu.VMEM((2 * blocks, 2 * BLOCK, NBLEN), BF16),
            pltpu.VMEM((2 * blocks, 2 * BLOCK, NBLEN), BF16),
            pltpu.VMEM((2 * blocks, 2, NBLEN, PAIR), BF16),
            pltpu.VMEM((2, NBLEN, PAIR), F32),
            pltpu.VMEM((8, 128), jnp.int32),
            pltpu.SMEM((8, 128), jnp.int32),
            pltpu.SemaphoreType.DMA((chunks,)),
            pltpu.SemaphoreType.DMA((6 * chunks,)),
            pltpu.SemaphoreType.DMA((6 * chunks,)),
            pltpu.SemaphoreType.DMA((1,)),
        ],
        compiler_params=pltpu.CompilerParams(
            collective_id=0, has_side_effects=True, vmem_limit_bytes=54 * MIB
        ),
    )(entries, slots, queries, grads, pool)


def finish_kernel(
    entries, context, grad_queries, early_sums, returned, context_out, grad_out, pool_grads, total, low, sems
):
    early = early_sums.shape[0]
    last = pl.ds(early * PAIR, PAIR)
    moves = [
        pltpu.make_async_copy(context, context_out, sems.at[0]),
        pltpu.make_async_copy(grad_queries, grad_out, sems.at[1]),
    ]
    for c in range(early):
        moves.append(
            pltpu.make_async_copy(
                early_sums.at[c], pool_grads.at[:, :, :, pl.ds(c * PAIR, PAIR)], sems.at[3 + c]
            )
        )
    for move in moves:
        move.start()
    total[...] = jnp.zeros_like(total)

    def step(e, carry):
        total[entries[0, e]] += returned[e].astype(F32)
        return carry

    lax.fori_loop(0, returned.shape[0], step, 0)
    low[...] = total[...].astype(BF16)
    moves.append(pltpu.make_async_copy(low, pool_grads.at[:, :, :, last], sems.at[2]))
    moves[-1].start()
    for move in moves:
        move.wait()


def finish(entries, context, grad_queries, early_sums, returned, pool_shape):
    tokens = jax.ShapeDtypeStruct(context.shape, context.dtype)
    part = pool_shape[:-1] + (PAIR,)
    return pl.pallas_call(
        finish_kernel,
        out_shape=(tokens, tokens, jax.ShapeDtypeStruct(pool_shape, BF16)),
        in_specs=[SCALAR] + [IN_VMEM] * 4,
        out_specs=(ANY, ANY, ANY),
        scratch_shapes=[
            pltpu.VMEM(part, F32),
            pltpu.VMEM(part, BF16),
            pltpu.SemaphoreType.DMA((3 + early_sums.shape[0],)),
        ],
        compiler_params=pltpu.CompilerParams(vmem_limit_bytes=16 * MIB),
    )(entries, context, grad_queries, early_sums, returned)


def local(enc_count, seq_count, queries, kv_pool, send_lists, block_slots, grad_context):
    entries = send_lists.reshape(1, -1)
    slots = block_slots[0].T
    context, grad_queries, early_sums, returned = everything(
        enc_count, seq_count, entries, slots, queries[0], grad_context[0], kv_pool
    )
    context, grad_queries, pool_grads = finish(
        entries, context, grad_queries, early_sums, returned, kv_pool.shape
    )
    return context[None], grad_queries[None], pool_grads


def solution(mesh):
    in_specs = (
        P("enc", "seq", None),
        P("enc", None, None, "seq"),
        P("enc", None, None),
        P("enc", None, None),
        P("enc", "seq", None),
    )
    out_specs = (P("enc", "seq", None), P("enc", "seq", None), P("enc", None, None, "seq"))
    body = functools.partial(local, mesh.shape["enc"], mesh.shape["seq"])
    return jax.shard_map(body, mesh=mesh, in_specs=in_specs, out_specs=out_specs, check_vma=False)
```

```python
import functools

import jax
import jax.numpy as jnp
from jax import lax
from jax.experimental import pallas as pl
from jax.experimental.pallas import tpu as pltpu
from jax.sharding import PartitionSpec as P

DH = 128
BLOCK = 64
NBLEN = 128
PAIR = 2 * DH
MESH = pl.DeviceIdType.MESH
ANY = pl.BlockSpec(memory_space=pl.ANY)
IN_VMEM = pl.BlockSpec(memory_space=pltpu.VMEM)
SCALAR = pl.BlockSpec(memory_space=pltpu.SMEM)
MIB = 1 << 20
SPLIT = 1
NT = (((1,), (1,)), ((), ()))
TN = (((0,), (0,)), ((), ()))
F32 = jnp.float32
BF16 = jnp.bfloat16


def sort_uses(slots, rank_ref, first_row):
    neighbours, blocks = slots.shape
    uses = neighbours * blocks
    lane = lax.broadcasted_iota(jnp.int32, (uses, 128), 1)
    row = lax.broadcasted_iota(jnp.int32, (uses, 128), 0)
    along_lanes = jnp.full((uses, 128), uses * 128, jnp.int32)
    along_rows = jnp.zeros((uses, 128), jnp.int32)
    slot_rows = jnp.zeros((uses, 128), jnp.int32)
    for n in range(neighbours):

        def put(b, carry, n=n):
            along_lanes, along_rows, slot_rows = carry
            use = n * blocks + b
            key = slots[n, b] * uses + use
            along_lanes = jnp.where(lane == use, key, along_lanes)
            along_rows = jnp.where(row == use, key, along_rows)
            slot_rows = jnp.where(row == use, slots[n, b], slot_rows)
            return along_lanes, along_rows, slot_rows

        along_lanes, along_rows, slot_rows = lax.fori_loop(
            0, blocks, put, (along_lanes, along_rows, slot_rows)
        )
    rank = jnp.sum((along_lanes < along_rows).astype(jnp.int32), axis=1, keepdims=True)
    order = jnp.sum(jnp.where(rank == lane, row, 0), axis=0, keepdims=True)
    ends = jnp.sum((slot_rows <= lane).astype(jnp.int32), axis=0, keepdims=True) - 1
    rank_ref[first_row : first_row + 1, :] = order
    rank_ref[first_row + 1 : first_row + 2, :] = ends


def block_pass(slots, queries, grads, received, out, query_grads, wide_q, wide_g, probs_kept, scores_kept):
    blocks = queries.shape[0] // BLOCK
    scale = DH ** (-0.5)
    is_last = lax.broadcasted_iota(jnp.int32, (BLOCK, PAIR), 0) == BLOCK - 1
    is_first_head = lax.broadcasted_iota(jnp.int32, (BLOCK, PAIR), 1) < DH

    def moved(ref, b):
        here = ref[pl.ds(pl.multiple_of(b * BLOCK, BLOCK), BLOCK), :].astype(F32)
        after = jnp.minimum(b + 1, blocks - 1)
        later = ref[pl.ds(pl.multiple_of(after * BLOCK, BLOCK), BLOCK), :].astype(F32)
        later = jnp.where(b + 1 < blocks, later, 0.0)
        row = jnp.where(is_last, here, later)
        pair = [jnp.where(is_first_head, row, 0.0), jnp.where(is_first_head, 0.0, row)]
        return jnp.concatenate(pair, axis=0).astype(BF16)

    def both(wide):
        return jnp.where(is_first_head, wide[:BLOCK], wide[BLOCK:])

    def step(b, carry):
        last_out, last_grad = carry
        first, second = slots[0, b], slots[1, b]
        query, grad = moved(queries, b), moved(grads, b)
        wide_q[b] = query
        wide_g[b] = grad
        keys = jnp.concatenate([received[first, 0], received[second, 0]], axis=0)
        values = jnp.concatenate([received[first, 1], received[second, 1]], axis=0)
        scores = lax.dot_general(query, keys, NT, preferred_element_type=F32) * scale
        weights = jnp.exp(scores - jnp.max(scores, axis=-1, keepdims=True))
        probs = weights / jnp.sum(weights, axis=-1, keepdims=True)
        probs_low = probs.astype(BF16)
        new_out = both(jnp.dot(probs_low, values, preferred_element_type=F32))
        grad_probs = lax.dot_general(grad, values, NT, preferred_element_type=F32)
        inner = jnp.sum(probs * grad_probs, axis=-1, keepdims=True)
        grad_scores = (probs * (grad_probs - inner) * scale).astype(BF16)
        new_grad = both(jnp.dot(grad_scores, keys, preferred_element_type=F32))
        for n in range(2):
            probs_kept[n * blocks + b] = probs_low[:, n * NBLEN : (n + 1) * NBLEN]
            scores_kept[n * blocks + b] = grad_scores[:, n * NBLEN : (n + 1) * NBLEN]
        here = pl.ds(pl.multiple_of(b * BLOCK, BLOCK), BLOCK)
        out[here, :] = jnp.where(is_last, new_out, last_out).astype(BF16)
        query_grads[here, :] = jnp.where(is_last, new_grad, last_grad).astype(BF16)
        return new_out, new_grad

    zeros = jnp.zeros((BLOCK, PAIR), F32)
    lax.fori_loop(0, blocks, step, (zeros, zeros), unroll=2)


def slot_pass(slots, ranks, wide_q, wide_g, probs_kept, scores_kept, running, sums, slot_grads):
    neighbours, blocks = slots.shape
    sums[...] = jnp.zeros_like(sums)

    def step(u, before):
        use = ranks[0, u]
        neighbour = lax.div(use, blocks)
        block = use - neighbour * blocks
        slot = slots[neighbour, block]
        for part, (kept, wide) in enumerate(((scores_kept, wide_q), (probs_kept, wide_g))):
            new = lax.dot_general(kept[use], wide[block], TN, preferred_element_type=F32)
            new = new.astype(BF16).astype(F32)
            new = jnp.where(slot != before, 0.0, sums[part]) + new
            sums[part] = new
            running[u, part] = new.astype(BF16)
        return slot

    def pick(s, carry):
        slot_grads[s] = running[ranks[1, s]]
        return carry

    lax.fori_loop(0, neighbours * blocks, step, -1, unroll=2)
    lax.fori_loop(0, slot_grads.shape[0], pick, 0)


def owner_pass(entries, ranks, returned, running, sums, store):
    def step(place, before):
        sender = ranks[2, place]
        entry = entries[0, sender]
        for part in range(2):
            new = returned[sender, part].astype(F32)
            new = jnp.where(entry != before, 0.0, sums[part]) + new
            sums[part] = new
            running[place, part] = new.astype(BF16)
        return entry

    sums[...] = jnp.zeros_like(sums)
    lax.fori_loop(0, entries.shape[1], step, -1)
    store(lambda entry: running[ranks[3, entry]])


def everything_kernel(
    enc_count, seq_count, chunks,
    entries, slots, queries, grads, pool, context, grad_queries, early_sums, last_returned,
    *scratch,
):
    take = iter(scratch)
    per_chunk = [[next(take) for _ in range(9)] for _ in range(chunks - 1)]
    per_chunk.append([next(take) for _ in range(8)] + [last_returned])
    wide_q, wide_g, probs_kept, scores_kept, running, sums = [next(take) for _ in range(6)]
    rank_ref, ranks, pool_sems, send_sems, recv_sems, rank_sem = [next(take) for _ in range(6)]

    enc_here, seq_here = lax.axis_index("enc"), lax.axis_index("seq")
    rows = queries.shape[0]
    width = pool.shape[-1]
    mine = pl.ds(pl.multiple_of(seq_here * rows, rows), rows)

    def peer_of(here, k, count):
        return lax.rem(here + k, count)

    loads = []
    for c in range(chunks):
        own = per_chunk[c][0]
        loads.append(pltpu.make_async_copy(pool.at[:, :, :, pl.ds(c * PAIR, PAIR)], own, pool_sems.at[c]))
        loads[-1].start()

    barrier = pltpu.get_barrier_semaphore()

    def greet_enc(k, carry):
        pl.semaphore_signal(
            barrier, inc=1, device_id={"enc": peer_of(enc_here, k, enc_count)}, device_id_type=MESH
        )
        return carry

    def greet_seq(k, carry):
        pl.semaphore_signal(
            barrier, inc=1, device_id={"seq": peer_of(seq_here, k, seq_count)}, device_id_type=MESH
        )
        return carry

    lax.fori_loop(1, enc_count, greet_enc, 0)
    lax.fori_loop(1, seq_count, greet_seq, 0)

    def pick(c):
        loads[c].wait()
        own, outgoing = per_chunk[c][0], per_chunk[c][1]

        def body(e, carry):
            outgoing[e] = own[entries[0, e]]
            return carry

        lax.fori_loop(0, enc_count, body, 0)

    def exchange(group, axis, here, count, source_of, target_of):
        def body(i, carry):
            k = count // 2 + (1 - 2 * lax.rem(i, 2)) * lax.div(i + 1, 2)
            peer = peer_of(here, k, count)
            pltpu.make_async_remote_copy(
                src_ref=source_of(peer),
                dst_ref=target_of(here),
                send_sem=send_sems.at[group],
                recv_sem=recv_sems.at[group],
                device_id={axis: peer},
                device_id_type=MESH,
            ).start()
            return carry

        lax.fori_loop(0, count - 1, body, 0)
        pltpu.make_async_copy(source_of(here), target_of(here), recv_sems.at[group]).start()

    def cut(c, p):
        return pl.ds(pl.multiple_of(p * width + c * PAIR, PAIR), PAIR)

    def token_rows(p):
        return pl.ds(pl.multiple_of(p * rows, rows), rows)

    def fetch(c):
        own, outgoing, arrived = per_chunk[c][:3]
        exchange(6 * c, "enc", enc_here, enc_count, lambda p: outgoing.at[p], lambda p: arrived.at[p])

    def to_heads(c):
        head_queries, head_grads = per_chunk[c][3:5]
        for n, (source, target) in enumerate(((queries, head_queries), (grads, head_grads))):
            exchange(
                6 * c + 1 + n, "seq", seq_here, seq_count,
                lambda p, source=source: source.at[:, cut(c, p)],
                lambda p, target=target: target.at[token_rows(p), :],
            )

    def to_tokens(c):
        out, query_grads = per_chunk[c][5:7]
        for n, (source, target) in enumerate(((out, context), (query_grads, grad_queries))):
            exchange(
                6 * c + 3 + n, "seq", seq_here, seq_count,
                lambda p, source=source: source.at[token_rows(p), :],
                lambda p, target=target: target.at[:, cut(c, p)],
            )

    def give_back(c):
        slot_grads, returned = per_chunk[c][7:9]
        exchange(
            6 * c + 5, "enc", enc_here, enc_count,
            lambda p: slot_grads.at[p], lambda p: returned.at[p],
        )

    def whole(ref, sem):
        pltpu.make_async_copy(ref, ref, sem).wait()

    def sent(group, ref, count):
        part = ref.at[pl.ds(0, ref.shape[0] // count * (count - 1))]
        whole(part, send_sems.at[group])

    def arrive(group, ref):
        whole(ref, recv_sems.at[group])

    def compute(c):
        _, _, arrived, head_queries, head_grads, out, query_grads, slot_grads, returned = per_chunk[c]
        arrive(6 * c, arrived)
        arrive(6 * c + 1, head_queries)
        arrive(6 * c + 2, head_grads)
        block_pass(
            slots, head_queries, head_grads, arrived, out, query_grads,
            wide_q, wide_g, probs_kept, scores_kept,
        )
        to_tokens(c)
        slot_pass(
            slots, ranks, wide_q, wide_g, probs_kept, scores_kept, running, sums, slot_grads
        )

    pick(0)
    pl.semaphore_wait(barrier, enc_count + seq_count - 2)
    fetch(0)
    to_heads(0)
    for c in range(1, chunks):
        pick(c)
    sort_uses(slots, rank_ref, 0)
    sort_uses(entries, rank_ref, 2)
    copy = pltpu.make_async_copy(rank_ref, ranks, rank_sem.at[0])
    copy.start()
    copy.wait()
    for c in range(chunks):
        sent(6 * c, per_chunk[c][1], enc_count)
        if c + 1 < chunks:
            fetch(c + 1)
            to_heads(c + 1)
        if c > 0:
            give_back(c - 1)
        compute(c)
    give_back(chunks - 1)

    for c in range(chunks):
        _, _, arrived, head_queries, head_grads, out, query_grads, slot_grads, returned = per_chunk[c]
        sent(6 * c + 1, head_queries, seq_count)
        sent(6 * c + 2, head_grads, seq_count)
        sent(6 * c + 3, out, seq_count)
        sent(6 * c + 4, query_grads, seq_count)
        sent(6 * c + 5, slot_grads, enc_count)
        arrive(6 * c + 3, out)
        arrive(6 * c + 4, query_grads)
        arrive(6 * c + 5, returned)

        if c + 1 < chunks:

            def store(value, c=c):
                def body(entry, carry):
                    early_sums[c, entry] = value(entry)
                    return carry

                lax.fori_loop(0, pool.shape[0], body, 0)

            owner_pass(entries, ranks, returned, running, sums, store)


def everything(enc_count, seq_count, entries, slots, queries, grads, pool):
    rows = queries.shape[0]
    held, _, _, width = pool.shape
    chunks = width // PAIR
    length = rows * seq_count
    blocks = length // BLOCK
    tokens = pltpu.VMEM(queries.shape, queries.dtype)

    def entry_buffer(count):
        return pltpu.VMEM((count, 2, NBLEN, PAIR), BF16)

    heads = pltpu.VMEM((length, PAIR), BF16)
    chunk_shapes = [
        entry_buffer(held), entry_buffer(enc_count), entry_buffer(enc_count),
        heads, heads, heads, heads, entry_buffer(enc_count), entry_buffer(enc_count),
    ]
    return pl.pallas_call(
        functools.partial(everything_kernel, enc_count, seq_count, chunks),
        out_shape=(
            tokens,
            tokens,
            pltpu.VMEM((chunks - 1, held, 2, NBLEN, PAIR), pool.dtype),
            pltpu.VMEM((enc_count, 2, NBLEN, PAIR), pool.dtype),
        ),
        in_specs=[SCALAR] * 2 + [ANY] * 3,
        out_specs=(ANY, ANY, IN_VMEM, IN_VMEM),
        scratch_shapes=chunk_shapes * (chunks - 1)
        + chunk_shapes[:8]
        + [
            pltpu.VMEM((blocks, 2 * BLOCK, PAIR), BF16),
            pltpu.VMEM((blocks, 2 * BLOCK, PAIR), BF16),
            pltpu.VMEM((2 * blocks, 2 * BLOCK, NBLEN), BF16),
            pltpu.VMEM((2 * blocks, 2 * BLOCK, NBLEN), BF16),
            pltpu.VMEM((2 * blocks, 2, NBLEN, PAIR), BF16),
            pltpu.VMEM((2, NBLEN, PAIR), F32),
            pltpu.VMEM((8, 128), jnp.int32),
            pltpu.SMEM((8, 128), jnp.int32),
            pltpu.SemaphoreType.DMA((chunks,)),
            pltpu.SemaphoreType.DMA((6 * chunks,)),
            pltpu.SemaphoreType.DMA((6 * chunks,)),
            pltpu.SemaphoreType.DMA((1,)),
        ],
        compiler_params=pltpu.CompilerParams(
            collective_id=0, has_side_effects=True, vmem_limit_bytes=48 * MIB
        ),
    )(entries, slots, queries, grads, pool)


def finish_kernel(
    entries_far, context, grad_queries, early_sums, returned, context_out, grad_out, pool_grads,
    entries, total, low, sems,
):
    early = early_sums.shape[0]
    moves = []

    def move(source, target):
        moves.append(pltpu.make_async_copy(source, target, sems.at[len(moves)]))
        moves[-1].start()

    move(entries_far, entries)
    half = context.shape[0] // SPLIT
    for source, target in ((context, context_out), (grad_queries, grad_out)):
        for n in range(SPLIT):
            rows = pl.ds(n * half, half)
            move(source.at[rows, :], target.at[rows, :])
    for c in range(early):
        move(early_sums.at[c], pool_grads.at[:, :, :, pl.ds(c * PAIR, PAIR)])
    total[...] = jnp.zeros_like(total)
    moves.pop(0).wait()
    moves.insert(0, None)
    for part in range(2):

        def step(e, carry, part=part):
            total[part, entries[0, e]] += returned[e, part].astype(F32)
            return carry

        lax.fori_loop(0, returned.shape[0], step, 0)
        low[part] = total[part].astype(BF16)
        move(low.at[part], pool_grads.at[:, part, :, pl.ds(early * PAIR, PAIR)])
    for one in moves[1:]:
        one.wait()


def finish(entries, context, grad_queries, early_sums, returned, pool_shape):
    tokens = jax.ShapeDtypeStruct(context.shape, context.dtype)
    part = (pool_shape[1], pool_shape[0], pool_shape[2], PAIR)
    return pl.pallas_call(
        finish_kernel,
        out_shape=(tokens, tokens, jax.ShapeDtypeStruct(pool_shape, BF16)),
        in_specs=[ANY] + [IN_VMEM] * 4,
        out_specs=(ANY, ANY, ANY),
        scratch_shapes=[
            pltpu.SMEM(entries.shape, entries.dtype),
            pltpu.VMEM(part, F32),
            pltpu.VMEM(part, BF16),
            pltpu.SemaphoreType.DMA((3 + 2 * SPLIT + early_sums.shape[0],)),
        ],
        compiler_params=pltpu.CompilerParams(vmem_limit_bytes=16 * MIB),
    )(entries, context, grad_queries, early_sums, returned)


def local(enc_count, seq_count, queries, kv_pool, send_lists, block_slots, grad_context):
    entries = send_lists.reshape(1, -1)
    slots = block_slots[0].T
    context, grad_queries, early_sums, returned = everything(
        enc_count, seq_count, entries, slots, queries[0], grad_context[0], kv_pool
    )
    context, grad_queries, pool_grads = finish(
        entries, context, grad_queries, early_sums, returned, kv_pool.shape
    )
    return context[None], grad_queries[None], pool_grads


def solution(mesh):
    in_specs = (
        P("enc", "seq", None),
        P("enc", None, None, "seq"),
        P("enc", None, None),
        P("enc", None, None),
        P("enc", "seq", None),
    )
    out_specs = (P("enc", "seq", None), P("enc", "seq", None), P("enc", None, None, "seq"))
    body = functools.partial(local, mesh.shape["enc"], mesh.shape["seq"])
    return jax.shard_map(body, mesh=mesh, in_specs=in_specs, out_specs=out_specs, check_vma=False)
```

```python
import functools

import jax
import jax.numpy as jnp
from jax import lax
from jax.experimental import pallas as pl
from jax.experimental.pallas import tpu as pltpu
from jax.sharding import PartitionSpec as P

DH = 128
BLOCK = 64
NBLEN = 128
PAIR = 2 * DH
MESH = pl.DeviceIdType.MESH
ANY = pl.BlockSpec(memory_space=pl.ANY)
IN_VMEM = pl.BlockSpec(memory_space=pltpu.VMEM)
SCALAR = pl.BlockSpec(memory_space=pltpu.SMEM)
MIB = 1 << 20
SPLIT = 1
NT = (((1,), (1,)), ((), ()))
TN = (((0,), (0,)), ((), ()))
F32 = jnp.float32
BF16 = jnp.bfloat16


def sort_uses(slots, rank_ref, first_row):
    neighbours, blocks = slots.shape
    uses = neighbours * blocks
    lane = lax.broadcasted_iota(jnp.int32, (uses, 128), 1)
    row = lax.broadcasted_iota(jnp.int32, (uses, 128), 0)
    along_lanes = jnp.full((uses, 128), uses * 128, jnp.int32)
    along_rows = jnp.zeros((uses, 128), jnp.int32)
    slot_rows = jnp.zeros((uses, 128), jnp.int32)
    for n in range(neighbours):

        def put(b, carry, n=n):
            along_lanes, along_rows, slot_rows = carry
            use = n * blocks + b
            key = slots[n, b] * uses + use
            along_lanes = jnp.where(lane == use, key, along_lanes)
            along_rows = jnp.where(row == use, key, along_rows)
            slot_rows = jnp.where(row == use, slots[n, b], slot_rows)
            return along_lanes, along_rows, slot_rows

        along_lanes, along_rows, slot_rows = lax.fori_loop(
            0, blocks, put, (along_lanes, along_rows, slot_rows)
        )
    rank = jnp.sum((along_lanes < along_rows).astype(jnp.int32), axis=1, keepdims=True)
    order = jnp.sum(jnp.where(rank == lane, row, 0), axis=0, keepdims=True)
    ends = jnp.sum((slot_rows <= lane).astype(jnp.int32), axis=0, keepdims=True) - 1
    rank_ref[first_row : first_row + 1, :] = order
    rank_ref[first_row + 1 : first_row + 2, :] = ends


def block_pass(slots, queries, grads, received, out, query_grads, wide_q, wide_g, probs_kept, scores_kept):
    blocks = queries.shape[0] // BLOCK
    scale = DH ** (-0.5)
    is_last = lax.broadcasted_iota(jnp.int32, (BLOCK, PAIR), 0) == BLOCK - 1
    is_first_head = lax.broadcasted_iota(jnp.int32, (BLOCK, PAIR), 1) < DH

    def moved(ref, b):
        here = ref[pl.ds(pl.multiple_of(b * BLOCK, BLOCK), BLOCK), :].astype(F32)
        after = jnp.minimum(b + 1, blocks - 1)
        later = ref[pl.ds(pl.multiple_of(after * BLOCK, BLOCK), BLOCK), :].astype(F32)
        later = jnp.where(b + 1 < blocks, later, 0.0)
        row = jnp.where(is_last, here, later)
        pair = [jnp.where(is_first_head, row, 0.0), jnp.where(is_first_head, 0.0, row)]
        return jnp.concatenate(pair, axis=0).astype(BF16)

    def both(wide):
        return jnp.where(is_first_head, wide[:BLOCK], wide[BLOCK:])

    def step(b, carry):
        last_out, last_grad = carry
        first, second = slots[0, b], slots[1, b]
        query, grad = moved(queries, b), moved(grads, b)
        wide_q[b] = query
        wide_g[b] = grad
        keys = jnp.concatenate([received[first, 0], received[second, 0]], axis=0)
        values = jnp.concatenate([received[first, 1], received[second, 1]], axis=0)
        scores = lax.dot_general(query, keys, NT, preferred_element_type=F32) * scale
        weights = jnp.exp(scores - jnp.max(scores, axis=-1, keepdims=True))
        probs = weights / jnp.sum(weights, axis=-1, keepdims=True)
        probs_low = probs.astype(BF16)
        new_out = both(jnp.dot(probs_low, values, preferred_element_type=F32))
        grad_probs = lax.dot_general(grad, values, NT, preferred_element_type=F32)
        inner = jnp.sum(probs * grad_probs, axis=-1, keepdims=True)
        grad_scores = (probs * (grad_probs - inner) * scale).astype(BF16)
        new_grad = both(jnp.dot(grad_scores, keys, preferred_element_type=F32))
        for n in range(2):
            probs_kept[n * blocks + b] = probs_low[:, n * NBLEN : (n + 1) * NBLEN]
            scores_kept[n * blocks + b] = grad_scores[:, n * NBLEN : (n + 1) * NBLEN]
        here = pl.ds(pl.multiple_of(b * BLOCK, BLOCK), BLOCK)
        out[here, :] = jnp.where(is_last, new_out, last_out).astype(BF16)
        query_grads[here, :] = jnp.where(is_last, new_grad, last_grad).astype(BF16)
        return new_out, new_grad

    zeros = jnp.zeros((BLOCK, PAIR), F32)
    lax.fori_loop(0, blocks, step, (zeros, zeros), unroll=2)


def slot_pass(slots, ranks, wide_q, wide_g, probs_kept, scores_kept, running, sums, slot_grads):
    neighbours, blocks = slots.shape
    sums[...] = jnp.zeros_like(sums)

    def step(u, before):
        use = ranks[0, u]
        neighbour = lax.div(use, blocks)
        block = use - neighbour * blocks
        slot = slots[neighbour, block]
        for part, (kept, wide) in enumerate(((scores_kept, wide_q), (probs_kept, wide_g))):
            new = lax.dot_general(kept[use], wide[block], TN, preferred_element_type=F32)
            new = new.astype(BF16).astype(F32)
            new = jnp.where(slot != before, 0.0, sums[part]) + new
            sums[part] = new
            running[u, part] = new.astype(BF16)
        return slot

    def pick(s, carry):
        slot_grads[s] = running[ranks[1, s]]
        return carry

    lax.fori_loop(0, neighbours * blocks, step, -1, unroll=2)
    lax.fori_loop(0, slot_grads.shape[0], pick, 0)


def owner_pass(entries, ranks, returned, running, sums, store):
    def step(place, before):
        sender = ranks[2, place]
        entry = entries[0, sender]
        for part in range(2):
            new = returned[sender, part].astype(F32)
            new = jnp.where(entry != before, 0.0, sums[part]) + new
            sums[part] = new
            running[place, part] = new.astype(BF16)
        return entry

    sums[...] = jnp.zeros_like(sums)
    lax.fori_loop(0, entries.shape[1], step, -1)
    store(lambda entry: running[ranks[3, entry]])


def everything_kernel(
    enc_count, seq_count, chunks,
    entries_far, slots_far, queries, grads, pool, context, grad_queries, early_sums, last_returned,
    *scratch,
):
    take = iter(scratch)
    per_chunk = [[next(take) for _ in range(9)] for _ in range(chunks - 1)]
    per_chunk.append([next(take) for _ in range(8)] + [last_returned])
    wide_q, wide_g, probs_kept, scores_kept, running, sums = [next(take) for _ in range(6)]
    rank_ref, ranks, pool_sems, send_sems, recv_sems, rank_sem = [next(take) for _ in range(6)]
    entries, slots, list_sems = [next(take) for _ in range(3)]

    enc_here, seq_here = lax.axis_index("enc"), lax.axis_index("seq")
    rows = queries.shape[0]
    width = pool.shape[-1]
    mine = pl.ds(pl.multiple_of(seq_here * rows, rows), rows)

    def peer_of(here, k, count):
        return lax.rem(here + k, count)

    loads = []
    for c in range(chunks):
        own = per_chunk[c][0]
        loads.append(pltpu.make_async_copy(pool.at[:, :, :, pl.ds(c * PAIR, PAIR)], own, pool_sems.at[c]))
        loads[-1].start()

    lists = [
        pltpu.make_async_copy(entries_far, entries, list_sems.at[0]),
        pltpu.make_async_copy(slots_far, slots, list_sems.at[1]),
    ]
    for one in lists:
        one.start()
    barrier = pltpu.get_barrier_semaphore()

    def greet_enc(k, carry):
        pl.semaphore_signal(
            barrier, inc=1, device_id={"enc": peer_of(enc_here, k, enc_count)}, device_id_type=MESH
        )
        return carry

    def greet_seq(k, carry):
        pl.semaphore_signal(
            barrier, inc=1, device_id={"seq": peer_of(seq_here, k, seq_count)}, device_id_type=MESH
        )
        return carry

    lax.fori_loop(1, enc_count, greet_enc, 0)
    lax.fori_loop(1, seq_count, greet_seq, 0)

    def pick(c):
        loads[c].wait()
        own, outgoing = per_chunk[c][0], per_chunk[c][1]

        def body(e, carry):
            outgoing[e] = own[entries[0, e]]
            return carry

        lax.fori_loop(0, enc_count, body, 0)

    def exchange(group, axis, here, count, source_of, target_of):
        def body(i, carry):
            k = count // 2 + (1 - 2 * lax.rem(i, 2)) * lax.div(i + 1, 2)
            peer = peer_of(here, k, count)
            pltpu.make_async_remote_copy(
                src_ref=source_of(peer),
                dst_ref=target_of(here),
                send_sem=send_sems.at[group],
                recv_sem=recv_sems.at[group],
                device_id={axis: peer},
                device_id_type=MESH,
            ).start()
            return carry

        lax.fori_loop(0, count - 1, body, 0)
        pltpu.make_async_copy(source_of(here), target_of(here), recv_sems.at[group]).start()

    def cut(c, p):
        return pl.ds(pl.multiple_of(p * width + c * PAIR, PAIR), PAIR)

    def token_rows(p):
        return pl.ds(pl.multiple_of(p * rows, rows), rows)

    def fetch(c):
        own, outgoing, arrived = per_chunk[c][:3]
        exchange(6 * c, "enc", enc_here, enc_count, lambda p: outgoing.at[p], lambda p: arrived.at[p])

    def to_heads(c):
        head_queries, head_grads = per_chunk[c][3:5]
        for n, (source, target) in enumerate(((queries, head_queries), (grads, head_grads))):
            exchange(
                6 * c + 1 + n, "seq", seq_here, seq_count,
                lambda p, source=source: source.at[:, cut(c, p)],
                lambda p, target=target: target.at[token_rows(p), :],
            )

    def to_tokens(c):
        out, query_grads = per_chunk[c][5:7]
        for n, (source, target) in enumerate(((out, context), (query_grads, grad_queries))):
            exchange(
                6 * c + 3 + n, "seq", seq_here, seq_count,
                lambda p, source=source: source.at[token_rows(p), :],
                lambda p, target=target: target.at[:, cut(c, p)],
            )

    def give_back(c):
        slot_grads, returned = per_chunk[c][7:9]
        exchange(
            6 * c + 5, "enc", enc_here, enc_count,
            lambda p: slot_grads.at[p], lambda p: returned.at[p],
        )

    def whole(ref, sem):
        pltpu.make_async_copy(ref, ref, sem).wait()

    def sent(group, ref, count):
        part = ref.at[pl.ds(0, ref.shape[0] // count * (count - 1))]
        whole(part, send_sems.at[group])

    def arrive(group, ref):
        whole(ref, recv_sems.at[group])

    def compute(c):
        _, _, arrived, head_queries, head_grads, out, query_grads, slot_grads, returned = per_chunk[c]
        arrive(6 * c, arrived)
        arrive(6 * c + 1, head_queries)
        arrive(6 * c + 2, head_grads)
        block_pass(
            slots, head_queries, head_grads, arrived, out, query_grads,
            wide_q, wide_g, probs_kept, scores_kept,
        )
        to_tokens(c)
        slot_pass(
            slots, ranks, wide_q, wide_g, probs_kept, scores_kept, running, sums, slot_grads
        )

    for one in lists:
        one.wait()
    pick(0)
    pl.semaphore_wait(barrier, enc_count + seq_count - 2)
    fetch(0)
    to_heads(0)
    for c in range(1, chunks):
        pick(c)
    sort_uses(slots, rank_ref, 0)
    sort_uses(entries, rank_ref, 2)
    copy = pltpu.make_async_copy(rank_ref, ranks, rank_sem.at[0])
    copy.start()
    copy.wait()
    for c in range(chunks):
        sent(6 * c, per_chunk[c][1], enc_count)
        if c + 1 < chunks:
            fetch(c + 1)
            to_heads(c + 1)
        if c > 0:
            give_back(c - 1)
        compute(c)
    give_back(chunks - 1)

    for c in range(chunks):
        _, _, arrived, head_queries, head_grads, out, query_grads, slot_grads, returned = per_chunk[c]
        sent(6 * c + 1, head_queries, seq_count)
        sent(6 * c + 2, head_grads, seq_count)
        sent(6 * c + 3, out, seq_count)
        sent(6 * c + 4, query_grads, seq_count)
        sent(6 * c + 5, slot_grads, enc_count)
        arrive(6 * c + 3, out)
        arrive(6 * c + 4, query_grads)
        arrive(6 * c + 5, returned)

        if c + 1 < chunks:

            def store(value, c=c):
                def body(entry, carry):
                    early_sums[c, entry] = value(entry)
                    return carry

                lax.fori_loop(0, pool.shape[0], body, 0)

            owner_pass(entries, ranks, returned, running, sums, store)


def everything(enc_count, seq_count, entries, slots, queries, grads, pool):
    rows = queries.shape[0]
    held, _, _, width = pool.shape
    chunks = width // PAIR
    length = rows * seq_count
    blocks = length // BLOCK
    tokens = pltpu.VMEM(queries.shape, queries.dtype)

    def entry_buffer(count):
        return pltpu.VMEM((count, 2, NBLEN, PAIR), BF16)

    heads = pltpu.VMEM((length, PAIR), BF16)
    chunk_shapes = [
        entry_buffer(held), entry_buffer(enc_count), entry_buffer(enc_count),
        heads, heads, heads, heads, entry_buffer(enc_count), entry_buffer(enc_count),
    ]
    return pl.pallas_call(
        functools.partial(everything_kernel, enc_count, seq_count, chunks),
        out_shape=(
            tokens,
            tokens,
            pltpu.VMEM((chunks - 1, held, 2, NBLEN, PAIR), pool.dtype),
            pltpu.VMEM((enc_count, 2, NBLEN, PAIR), pool.dtype),
        ),
        in_specs=[ANY] * 5,
        out_specs=(ANY, ANY, IN_VMEM, IN_VMEM),
        scratch_shapes=chunk_shapes * (chunks - 1)
        + chunk_shapes[:8]
        + [
            pltpu.VMEM((blocks, 2 * BLOCK, PAIR), BF16),
            pltpu.VMEM((blocks, 2 * BLOCK, PAIR), BF16),
            pltpu.VMEM((2 * blocks, 2 * BLOCK, NBLEN), BF16),
            pltpu.VMEM((2 * blocks, 2 * BLOCK, NBLEN), BF16),
            pltpu.VMEM((2 * blocks, 2, NBLEN, PAIR), BF16),
            pltpu.VMEM((2, NBLEN, PAIR), F32),
            pltpu.VMEM((8, 128), jnp.int32),
            pltpu.SMEM((8, 128), jnp.int32),
            pltpu.SemaphoreType.DMA((chunks,)),
            pltpu.SemaphoreType.DMA((6 * chunks,)),
            pltpu.SemaphoreType.DMA((6 * chunks,)),
            pltpu.SemaphoreType.DMA((1,)),
            pltpu.SMEM(entries.shape, entries.dtype),
            pltpu.SMEM(slots.shape, slots.dtype),
            pltpu.SemaphoreType.DMA((2,)),
        ],
        compiler_params=pltpu.CompilerParams(
            collective_id=0, has_side_effects=True, vmem_limit_bytes=48 * MIB
        ),
    )(entries, slots, queries, grads, pool)


def finish_kernel(
    entries_far, context, grad_queries, early_sums, returned, context_out, grad_out, pool_grads,
    entries, total, low, sems,
):
    early = early_sums.shape[0]
    moves = []

    def move(source, target):
        moves.append(pltpu.make_async_copy(source, target, sems.at[len(moves)]))
        moves[-1].start()

    move(entries_far, entries)
    half = context.shape[0] // SPLIT
    for source, target in ((context, context_out), (grad_queries, grad_out)):
        for n in range(SPLIT):
            rows = pl.ds(n * half, half)
            move(source.at[rows, :], target.at[rows, :])
    for c in range(early):
        move(early_sums.at[c], pool_grads.at[:, :, :, pl.ds(c * PAIR, PAIR)])
    total[...] = jnp.zeros_like(total)
    moves.pop(0).wait()
    moves.insert(0, None)
    for part in range(2):

        def step(e, carry, part=part):
            total[part, entries[0, e]] += returned[e, part].astype(F32)
            return carry

        lax.fori_loop(0, returned.shape[0], step, 0)
        low[part] = total[part].astype(BF16)
        move(low.at[part], pool_grads.at[:, part, :, pl.ds(early * PAIR, PAIR)])
    for one in moves[1:]:
        one.wait()


def finish(entries, context, grad_queries, early_sums, returned, pool_shape):
    tokens = jax.ShapeDtypeStruct(context.shape, context.dtype)
    part = (pool_shape[1], pool_shape[0], pool_shape[2], PAIR)
    return pl.pallas_call(
        finish_kernel,
        out_shape=(tokens, tokens, jax.ShapeDtypeStruct(pool_shape, BF16)),
        in_specs=[ANY] + [IN_VMEM] * 4,
        out_specs=(ANY, ANY, ANY),
        scratch_shapes=[
            pltpu.SMEM(entries.shape, entries.dtype),
            pltpu.VMEM(part, F32),
            pltpu.VMEM(part, BF16),
            pltpu.SemaphoreType.DMA((3 + 2 * SPLIT + early_sums.shape[0],)),
        ],
        compiler_params=pltpu.CompilerParams(vmem_limit_bytes=16 * MIB),
    )(entries, context, grad_queries, early_sums, returned)


def local(enc_count, seq_count, queries, kv_pool, send_lists, block_slots, grad_context):
    entries = send_lists.reshape(1, -1)
    slots = block_slots[0].T
    context, grad_queries, early_sums, returned = everything(
        enc_count, seq_count, entries, slots, queries[0], grad_context[0], kv_pool
    )
    context, grad_queries, pool_grads = finish(
        entries, context, grad_queries, early_sums, returned, kv_pool.shape
    )
    return context[None], grad_queries[None], pool_grads


def solution(mesh):
    in_specs = (
        P("enc", "seq", None),
        P("enc", None, None, "seq"),
        P("enc", None, None),
        P("enc", None, None),
        P("enc", "seq", None),
    )
    out_specs = (P("enc", "seq", None), P("enc", "seq", None), P("enc", None, None, "seq"))
    body = functools.partial(local, mesh.shape["enc"], mesh.shape["seq"])
    return jax.shard_map(body, mesh=mesh, in_specs=in_specs, out_specs=out_specs, check_vma=False)
```

```python
import functools

import jax
import jax.numpy as jnp
from jax import lax
from jax.experimental import pallas as pl
from jax.experimental.pallas import tpu as pltpu
from jax.sharding import PartitionSpec as P

DH = 128
BLOCK = 64
NBLEN = 128
PAIR = 2 * DH
MESH = pl.DeviceIdType.MESH
ANY = pl.BlockSpec(memory_space=pl.ANY)
IN_VMEM = pl.BlockSpec(memory_space=pltpu.VMEM)
SCALAR = pl.BlockSpec(memory_space=pltpu.SMEM)
MIB = 1 << 20
SPLIT = 1
NT = (((1,), (1,)), ((), ()))
TN = (((0,), (0,)), ((), ()))
F32 = jnp.float32
BF16 = jnp.bfloat16


def sort_uses(slots, rank_ref, first_row):
    neighbours, blocks = slots.shape
    uses = neighbours * blocks
    lane = lax.broadcasted_iota(jnp.int32, (uses, 128), 1)
    row = lax.broadcasted_iota(jnp.int32, (uses, 128), 0)
    along_lanes = jnp.full((uses, 128), uses * 128, jnp.int32)
    along_rows = jnp.zeros((uses, 128), jnp.int32)
    slot_rows = jnp.zeros((uses, 128), jnp.int32)
    for n in range(neighbours):

        def put(b, carry, n=n):
            along_lanes, along_rows, slot_rows = carry
            use = n * blocks + b
            key = slots[n, b] * uses + use
            along_lanes = jnp.where(lane == use, key, along_lanes)
            along_rows = jnp.where(row == use, key, along_rows)
            slot_rows = jnp.where(row == use, slots[n, b], slot_rows)
            return along_lanes, along_rows, slot_rows

        along_lanes, along_rows, slot_rows = lax.fori_loop(
            0, blocks, put, (along_lanes, along_rows, slot_rows)
        )
    rank = jnp.sum((along_lanes < along_rows).astype(jnp.int32), axis=1, keepdims=True)
    order = jnp.sum(jnp.where(rank == lane, row, 0), axis=0, keepdims=True)
    ends = jnp.sum((slot_rows <= lane).astype(jnp.int32), axis=0, keepdims=True) - 1
    rank_ref[first_row : first_row + 1, :] = order
    rank_ref[first_row + 1 : first_row + 2, :] = ends


def block_pass(slots, queries, grads, received, out, query_grads, wide_q, wide_g, probs_kept, scores_kept):
    blocks = queries.shape[0] // BLOCK
    scale = DH ** (-0.5)
    is_last = lax.broadcasted_iota(jnp.int32, (BLOCK, PAIR), 0) == BLOCK - 1
    is_first_head = lax.broadcasted_iota(jnp.int32, (BLOCK, PAIR), 1) < DH

    def moved(ref, b):
        here = ref[pl.ds(pl.multiple_of(b * BLOCK, BLOCK), BLOCK), :].astype(F32)
        after = jnp.minimum(b + 1, blocks - 1)
        later = ref[pl.ds(pl.multiple_of(after * BLOCK, BLOCK), BLOCK), :].astype(F32)
        later = jnp.where(b + 1 < blocks, later, 0.0)
        row = jnp.where(is_last, here, later)
        pair = [jnp.where(is_first_head, row, 0.0), jnp.where(is_first_head, 0.0, row)]
        return jnp.concatenate(pair, axis=0).astype(BF16)

    def both(wide):
        return jnp.where(is_first_head, wide[:BLOCK], wide[BLOCK:])

    def step(b, carry):
        last_out, last_grad = carry
        first, second = slots[0, b], slots[1, b]
        query, grad = moved(queries, b), moved(grads, b)
        wide_q[b] = query
        wide_g[b] = grad
        keys = jnp.concatenate([received[first, 0], received[second, 0]], axis=0)
        values = jnp.concatenate([received[first, 1], received[second, 1]], axis=0)
        scores = lax.dot_general(query, keys, NT, preferred_element_type=F32) * scale
        weights = jnp.exp(scores - jnp.max(scores, axis=-1, keepdims=True))
        probs = weights / jnp.sum(weights, axis=-1, keepdims=True)
        probs_low = probs.astype(BF16)
        new_out = both(jnp.dot(probs_low, values, preferred_element_type=F32))
        grad_probs = lax.dot_general(grad, values, NT, preferred_element_type=F32)
        inner = jnp.sum(probs * grad_probs, axis=-1, keepdims=True)
        grad_scores = (probs * (grad_probs - inner) * scale).astype(BF16)
        new_grad = both(jnp.dot(grad_scores, keys, preferred_element_type=F32))
        for n in range(2):
            probs_kept[n * blocks + b] = probs_low[:, n * NBLEN : (n + 1) * NBLEN]
            scores_kept[n * blocks + b] = grad_scores[:, n * NBLEN : (n + 1) * NBLEN]
        here = pl.ds(pl.multiple_of(b * BLOCK, BLOCK), BLOCK)
        out[here, :] = jnp.where(is_last, new_out, last_out).astype(BF16)
        query_grads[here, :] = jnp.where(is_last, new_grad, last_grad).astype(BF16)
        return new_out, new_grad

    zeros = jnp.zeros((BLOCK, PAIR), F32)
    lax.fori_loop(0, blocks, step, (zeros, zeros), unroll=2)


def slot_pass(slots, ranks, wide_q, wide_g, probs_kept, scores_kept, running, sums, slot_grads):
    neighbours, blocks = slots.shape
    sums[...] = jnp.zeros_like(sums)

    def step(u, before):
        use = ranks[0, u]
        neighbour = lax.div(use, blocks)
        block = use - neighbour * blocks
        slot = slots[neighbour, block]
        for part, (kept, wide) in enumerate(((scores_kept, wide_q), (probs_kept, wide_g))):
            new = lax.dot_general(kept[use], wide[block], TN, preferred_element_type=F32)
            new = new.astype(BF16).astype(F32)
            new = jnp.where(slot != before, 0.0, sums[part]) + new
            sums[part] = new
            running[u, part] = new.astype(BF16)
        return slot

    def pick(s, carry):
        slot_grads[s] = running[ranks[1, s]]
        return carry

    lax.fori_loop(0, neighbours * blocks, step, -1, unroll=2)
    lax.fori_loop(0, slot_grads.shape[0], pick, 0)


def owner_pass(entries, ranks, returned, running, sums, store):
    def step(place, before):
        sender = ranks[2, place]
        entry = entries[0, sender]
        for part in range(2):
            new = returned[sender, part].astype(F32)
            new = jnp.where(entry != before, 0.0, sums[part]) + new
            sums[part] = new
            running[place, part] = new.astype(BF16)
        return entry

    sums[...] = jnp.zeros_like(sums)
    lax.fori_loop(0, entries.shape[1], step, -1)
    store(lambda entry: running[ranks[3, entry]])


def everything_kernel(
    enc_count, seq_count, chunks,
    entries_far, slots_far, queries, grads, pool, context, grad_queries, early_sums, last_returned,
    *scratch,
):
    take = iter(scratch)
    per_chunk = [[next(take) for _ in range(9)] for _ in range(chunks - 1)]
    per_chunk.append([next(take) for _ in range(8)] + [last_returned])
    wide_q, wide_g, probs_kept, scores_kept, running, sums = [next(take) for _ in range(6)]
    rank_ref, ranks, pool_sems, send_sems, recv_sems, rank_sem = [next(take) for _ in range(6)]
    entries, slots, list_sems = [next(take) for _ in range(3)]

    enc_here, seq_here = lax.axis_index("enc"), lax.axis_index("seq")
    rows = queries.shape[0]
    width = pool.shape[-1]
    mine = pl.ds(pl.multiple_of(seq_here * rows, rows), rows)

    def peer_of(here, k, count):
        return lax.rem(here + k, count)

    def far_first(i, count):
        return count // 2 + (1 - 2 * lax.rem(i, 2)) * lax.div(i + 1, 2)

    barrier = pltpu.get_barrier_semaphore()

    def greet_enc(i, carry):
        k = far_first(i, enc_count)
        pl.semaphore_signal(
            barrier, inc=1, device_id={"enc": peer_of(enc_here, k, enc_count)}, device_id_type=MESH
        )
        return carry

    def greet_seq(i, carry):
        k = far_first(i, seq_count)
        pl.semaphore_signal(
            barrier, inc=1, device_id={"seq": peer_of(seq_here, k, seq_count)}, device_id_type=MESH
        )
        return carry

    lax.fori_loop(0, enc_count - 1, greet_enc, 0)
    lists = [
        pltpu.make_async_copy(entries_far, entries, list_sems.at[0]),
        pltpu.make_async_copy(slots_far, slots, list_sems.at[1]),
    ]
    for one in lists:
        one.start()
    loads = []
    for c in range(chunks):
        own = per_chunk[c][0]
        loads.append(pltpu.make_async_copy(pool.at[:, :, :, pl.ds(c * PAIR, PAIR)], own, pool_sems.at[c]))
        loads[-1].start()
    lax.fori_loop(0, seq_count - 1, greet_seq, 0)

    def pick(c):
        loads[c].wait()
        own, outgoing = per_chunk[c][0], per_chunk[c][1]

        def body(e, carry):
            outgoing[e] = own[entries[0, e]]
            return carry

        lax.fori_loop(0, enc_count, body, 0)

    def exchange(group, axis, here, count, source_of, target_of):
        def body(i, carry):
            k = far_first(i, count)
            peer = peer_of(here, k, count)
            pltpu.make_async_remote_copy(
                src_ref=source_of(peer),
                dst_ref=target_of(here),
                send_sem=send_sems.at[group],
                recv_sem=recv_sems.at[group],
                device_id={axis: peer},
                device_id_type=MESH,
            ).start()
            return carry

        lax.fori_loop(0, count - 1, body, 0)
        pltpu.make_async_copy(source_of(here), target_of(here), recv_sems.at[group]).start()

    def cut(c, p):
        return pl.ds(pl.multiple_of(p * width + c * PAIR, PAIR), PAIR)

    def token_rows(p):
        return pl.ds(pl.multiple_of(p * rows, rows), rows)

    def fetch(c):
        own, outgoing, arrived = per_chunk[c][:3]
        exchange(6 * c, "enc", enc_here, enc_count, lambda p: outgoing.at[p], lambda p: arrived.at[p])

    def to_heads(c):
        head_queries, head_grads = per_chunk[c][3:5]
        for n, (source, target) in enumerate(((queries, head_queries), (grads, head_grads))):
            exchange(
                6 * c + 1 + n, "seq", seq_here, seq_count,
                lambda p, source=source: source.at[:, cut(c, p)],
                lambda p, target=target: target.at[token_rows(p), :],
            )

    def to_tokens(c):
        out, query_grads = per_chunk[c][5:7]
        for n, (source, target) in enumerate(((out, context), (query_grads, grad_queries))):
            exchange(
                6 * c + 3 + n, "seq", seq_here, seq_count,
                lambda p, source=source: source.at[token_rows(p), :],
                lambda p, target=target: target.at[:, cut(c, p)],
            )

    def give_back(c):
        slot_grads, returned = per_chunk[c][7:9]
        exchange(
            6 * c + 5, "enc", enc_here, enc_count,
            lambda p: slot_grads.at[p], lambda p: returned.at[p],
        )

    def whole(ref, sem):
        pltpu.make_async_copy(ref, ref, sem).wait()

    def sent(group, ref, count):
        part = ref.at[pl.ds(0, ref.shape[0] // count * (count - 1))]
        whole(part, send_sems.at[group])

    def arrive(group, ref):
        whole(ref, recv_sems.at[group])

    def compute(c):
        _, _, arrived, head_queries, head_grads, out, query_grads, slot_grads, returned = per_chunk[c]
        arrive(6 * c, arrived)
        arrive(6 * c + 1, head_queries)
        arrive(6 * c + 2, head_grads)
        block_pass(
            slots, head_queries, head_grads, arrived, out, query_grads,
            wide_q, wide_g, probs_kept, scores_kept,
        )
        to_tokens(c)
        slot_pass(
            slots, ranks, wide_q, wide_g, probs_kept, scores_kept, running, sums, slot_grads
        )

    for one in lists:
        one.wait()
    pick(0)
    pl.semaphore_wait(barrier, enc_count + seq_count - 2)
    fetch(0)
    to_heads(0)
    for c in range(1, chunks):
        pick(c)
    sort_uses(slots, rank_ref, 0)
    sort_uses(entries, rank_ref, 2)
    copy = pltpu.make_async_copy(rank_ref, ranks, rank_sem.at[0])
    copy.start()
    copy.wait()
    for c in range(chunks):
        sent(6 * c, per_chunk[c][1], enc_count)
        if c + 1 < chunks:
            fetch(c + 1)
            to_heads(c + 1)
        if c > 0:
            give_back(c - 1)
        compute(c)
    give_back(chunks - 1)

    for c in range(chunks):
        _, _, arrived, head_queries, head_grads, out, query_grads, slot_grads, returned = per_chunk[c]
        sent(6 * c + 1, head_queries, seq_count)
        sent(6 * c + 2, head_grads, seq_count)
        sent(6 * c + 3, out, seq_count)
        sent(6 * c + 4, query_grads, seq_count)
        sent(6 * c + 5, slot_grads, enc_count)
        arrive(6 * c + 3, out)
        arrive(6 * c + 4, query_grads)
        arrive(6 * c + 5, returned)

        if c + 1 < chunks:

            def store(value, c=c):
                def body(entry, carry):
                    early_sums[c, entry] = value(entry)
                    return carry

                lax.fori_loop(0, pool.shape[0], body, 0)

            owner_pass(entries, ranks, returned, running, sums, store)


def everything(enc_count, seq_count, entries, slots, queries, grads, pool):
    rows = queries.shape[0]
    held, _, _, width = pool.shape
    chunks = width // PAIR
    length = rows * seq_count
    blocks = length // BLOCK
    tokens = pltpu.VMEM(queries.shape, queries.dtype)

    def entry_buffer(count):
        return pltpu.VMEM((count, 2, NBLEN, PAIR), BF16)

    heads = pltpu.VMEM((length, PAIR), BF16)
    chunk_shapes = [
        entry_buffer(held), entry_buffer(enc_count), entry_buffer(enc_count),
        heads, heads, heads, heads, entry_buffer(enc_count), entry_buffer(enc_count),
    ]
    return pl.pallas_call(
        functools.partial(everything_kernel, enc_count, seq_count, chunks),
        out_shape=(
            tokens,
            tokens,
            pltpu.VMEM((chunks - 1, held, 2, NBLEN, PAIR), pool.dtype),
            pltpu.VMEM((enc_count, 2, NBLEN, PAIR), pool.dtype),
        ),
        in_specs=[ANY] * 5,
        out_specs=(ANY, ANY, IN_VMEM, IN_VMEM),
        scratch_shapes=chunk_shapes * (chunks - 1)
        + chunk_shapes[:8]
        + [
            pltpu.VMEM((blocks, 2 * BLOCK, PAIR), BF16),
            pltpu.VMEM((blocks, 2 * BLOCK, PAIR), BF16),
            pltpu.VMEM((2 * blocks, 2 * BLOCK, NBLEN), BF16),
            pltpu.VMEM((2 * blocks, 2 * BLOCK, NBLEN), BF16),
            pltpu.VMEM((2 * blocks, 2, NBLEN, PAIR), BF16),
            pltpu.VMEM((2, NBLEN, PAIR), F32),
            pltpu.VMEM((8, 128), jnp.int32),
            pltpu.SMEM((8, 128), jnp.int32),
            pltpu.SemaphoreType.DMA((chunks,)),
            pltpu.SemaphoreType.DMA((6 * chunks,)),
            pltpu.SemaphoreType.DMA((6 * chunks,)),
            pltpu.SemaphoreType.DMA((1,)),
            pltpu.SMEM(entries.shape, entries.dtype),
            pltpu.SMEM(slots.shape, slots.dtype),
            pltpu.SemaphoreType.DMA((2,)),
        ],
        compiler_params=pltpu.CompilerParams(
            collective_id=0, has_side_effects=True, vmem_limit_bytes=48 * MIB
        ),
    )(entries, slots, queries, grads, pool)


def finish_kernel(
    entries_far, context, grad_queries, early_sums, returned, context_out, grad_out, pool_grads,
    entries, total, low, sems,
):
    early = early_sums.shape[0]
    moves = []

    def move(source, target):
        moves.append(pltpu.make_async_copy(source, target, sems.at[len(moves)]))
        moves[-1].start()

    move(entries_far, entries)
    half = context.shape[0] // SPLIT
    for source, target in ((context, context_out), (grad_queries, grad_out)):
        for n in range(SPLIT):
            rows = pl.ds(n * half, half)
            move(source.at[rows, :], target.at[rows, :])
    for c in range(early):
        move(early_sums.at[c], pool_grads.at[:, :, :, pl.ds(c * PAIR, PAIR)])
    total[...] = jnp.zeros_like(total)
    moves.pop(0).wait()
    moves.insert(0, None)
    for part in range(2):

        def step(e, carry, part=part):
            total[part, entries[0, e]] += returned[e, part].astype(F32)
            return carry

        lax.fori_loop(0, returned.shape[0], step, 0)
        low[part] = total[part].astype(BF16)
        move(low.at[part], pool_grads.at[:, part, :, pl.ds(early * PAIR, PAIR)])
    for one in moves[1:]:
        one.wait()


def finish(entries, context, grad_queries, early_sums, returned, pool_shape):
    tokens = jax.ShapeDtypeStruct(context.shape, context.dtype)
    part = (pool_shape[1], pool_shape[0], pool_shape[2], PAIR)
    return pl.pallas_call(
        finish_kernel,
        out_shape=(tokens, tokens, jax.ShapeDtypeStruct(pool_shape, BF16)),
        in_specs=[ANY] + [IN_VMEM] * 4,
        out_specs=(ANY, ANY, ANY),
        scratch_shapes=[
            pltpu.SMEM(entries.shape, entries.dtype),
            pltpu.VMEM(part, F32),
            pltpu.VMEM(part, BF16),
            pltpu.SemaphoreType.DMA((3 + 2 * SPLIT + early_sums.shape[0],)),
        ],
        compiler_params=pltpu.CompilerParams(vmem_limit_bytes=16 * MIB),
    )(entries, context, grad_queries, early_sums, returned)


def local(enc_count, seq_count, queries, kv_pool, send_lists, block_slots, grad_context):
    entries = send_lists.reshape(1, -1)
    slots = block_slots[0].T
    context, grad_queries, early_sums, returned = everything(
        enc_count, seq_count, entries, slots, queries[0], grad_context[0], kv_pool
    )
    context, grad_queries, pool_grads = finish(
        entries, context, grad_queries, early_sums, returned, kv_pool.shape
    )
    return context[None], grad_queries[None], pool_grads


def solution(mesh):
    in_specs = (
        P("enc", "seq", None),
        P("enc", None, None, "seq"),
        P("enc", None, None),
        P("enc", None, None),
        P("enc", "seq", None),
    )
    out_specs = (P("enc", "seq", None), P("enc", "seq", None), P("enc", None, None, "seq"))
    body = functools.partial(local, mesh.shape["enc"], mesh.shape["seq"])
    return jax.shard_map(body, mesh=mesh, in_specs=in_specs, out_specs=out_specs, check_vma=False)
```
